256 devices in a mesh: grp: 8 (over z), tp: 32 (over y, x, core).
Axes of the slice: x: 4, y: 4, z: 8, core: 2. Of those that a mesh axis runs over, the one named last changes fastest.
Arguments:
- hidden_in: bfloat16 [512, 4096], P('grp'), may hold values from -6 to 6
- norm_gain: float32 [4096], replicated, may hold values from 0.25 to 1.75
- head_weight: bfloat16 [4096, 128256], P('grp', 'tp'), may hold values from -1 to 1
- ffn_act: bfloat16 [512, 14336], P('grp', 'tp'), may hold values from -6 to 6
- labels: int32 [512], P('grp'), may hold values from 0 to 128255
- lengths: int32 [64], P('grp'), may hold values from 1 to 8
- proj_hidden: bfloat16 [4096, 64], replicated, may hold values from -0.09375 to 0.09375
- proj_vocab: bfloat16 [128256, 64], P('tp'), may hold values from -6 to 6
- proj_ffn: bfloat16 [14336, 64], P('tp'), may hold values from -0.046875 to 0.046875
- proj_down: bfloat16 [4096, 64], replicated, may hold values from -6 to 6
- store: bfloat16 [65536, 8192], P('grp', 'tp'), may hold values from -0.0625 to 0.0625
Outputs:
- scores: float32 [64, 65536], P('tp', 'grp')
The draws below stay inside these ranges and needn't reach their ends.
All inputs are finite; a program needn't handle non-finite values.
Results may differ from the reference program's by a relative error of at most 0.012.
Values may be sent and summed in bfloat16 or wider, within the bound.
No kernel may reach another device: no remote copies, remote signals or barrier semaphores. Data moves between devices by JAX's collectives and lax.ppermute only.
A program may use at most 64 MiB of HBM per device.

```python
import jax
import jax.numpy as jnp
from jax import lax

D = 4096
FF = 14336
V = 128256
RANK = 64
LEN = 8
TOKENS = 512
NQ = 64
NSTORE = 65536
F = 8192
N_GRP = 8


def planted_rows(key):
    base_key = jax.random.fold_in(key, 7717)
    key_list = jax.random.split(base_key, 6)
    chosen = jax.random.permutation(key_list[0], TOKENS // LEN)[:8]
    slot_rows = chosen.astype(jnp.int32) * LEN
    columns = jax.random.permutation(key_list[1], V)[:16].astype(jnp.int32)
    pattern = jnp.clip(jax.random.normal(key_list[2], (D, 8), jnp.float32), -6.0, 6.0)
    spare_values = jnp.clip(jax.random.normal(key_list[3], (D, 8), jnp.float32), -6.0, 6.0)
    offsets = jax.random.randint(key_list[4], (8,), 0, D)
    coords = jnp.arange(D, dtype=jnp.int32)[:, None]
    replaced = (coords - offsets[None, :]) % D < max(1, D // 160)
    partner = jnp.where(replaced, spare_values, pattern)
    strength = jax.random.uniform(key_list[5], (8,), jnp.float32, 0.6, 1.0)
    return (slot_rows, columns[:8], columns[8:], pattern, partner, strength)


def draw_head_weight(key, part):
    head_scale = (D // 9) ** (-0.5)
    planted_scale = 600.0 / D
    noise_values = jnp.clip(jax.random.normal(jax.random.fold_in(key, 31), (D, V), jnp.float32), -6.0, 6.0) * head_scale
    slot_rows, first_cols, second_cols, pattern, partner, strength = planted_rows(key)
    noise_values = noise_values.at[:, first_cols].set(planted_scale * pattern)
    noise_values = noise_values.at[:, second_cols].set(planted_scale * partner)
    return jnp.clip(noise_values, -1.0, 1.0).astype(jnp.bfloat16)


def draw_hidden_in(key, part):
    noise_values = jnp.clip(jax.random.normal(jax.random.fold_in(key, 53), (TOKENS, D), jnp.float32), -6.0, 6.0)
    slot_rows, first_cols, second_cols, pattern, partner, strength = planted_rows(key)
    mixing = jnp.sqrt(1.0 - strength * strength)
    aligned = strength[:, None] * pattern.T + mixing[:, None] * noise_values[slot_rows]
    noise_values = noise_values.at[slot_rows].set(jnp.clip(aligned, -6.0, 6.0))
    return noise_values.astype(jnp.bfloat16)


def with_ends(result, rng, least, high):
    dims = result.shape
    place = [jax.random.randint(jax.random.fold_in(rng, axis), (), 0, dims[axis]) for axis in range(len(dims))]
    result = result.at[tuple(place)].set(least)
    longest = dims.index(max(dims))
    place[longest] = (place[longest] + 1) % dims[longest]
    return result.at[tuple(place)].set(high)


def block_scale(rng, dims, cuts, smallest, top_value):
    def one(dim, parts):
        heights = jax.random.uniform(jax.random.fold_in(jax.random.fold_in(rng, 6), dim), (parts,), jnp.float32, smallest / len(cuts), top_value / len(cuts))
        return jnp.repeat(jnp.exp(heights), dims[dim] // parts).reshape((-1,) + (1,) * (len(dims) - dim - 1))

    gain = one(*cuts[0])
    for cut in cuts[1:]:
        gain = gain * one(*cut)
    return gain


def scatter_about(rng, dims, spread, limit, pieces=(), held_as=jnp.bfloat16):
    loudness = block_scale(rng, dims, pieces, -0.22, 0.18) if pieces else 1.0
    drawn = jax.random.normal(rng, dims, jnp.float32) * spread * loudness
    return jnp.minimum(jnp.maximum(drawn, -limit), limit).astype(held_as)


def setup_inputs(seed: int = 0) -> dict:
    key_of = jax.random.split(jax.random.key(seed), 12)
    return {
        "hidden_in": draw_hidden_in(jax.random.fold_in(key_of[11], 71), 0),
        "norm_gain": jnp.clip(1.0 + 0.15 * jax.random.normal(key_of[1], (D,), jnp.float32), 0.25, 1.75),
        "head_weight": draw_head_weight(jax.random.fold_in(key_of[11], 71), 0),
        "ffn_act": scatter_about(key_of[3], (TOKENS, FF), 1.0, 6.0, ((0, 8), (1, 32))),
        "labels": with_ends(jax.random.randint(key_of[4], (TOKENS,), 0, V), jax.random.fold_in(key_of[4], 1), 0, V - 1).astype(jnp.int32),
        "lengths": with_ends(jax.random.randint(key_of[5], (NQ,), 1, LEN + 1), jax.random.fold_in(key_of[5], 1), 1, LEN).astype(jnp.int32),
        "proj_hidden": scatter_about(key_of[6], (D, RANK), D ** -0.5, 0.09375),
        "proj_vocab": scatter_about(key_of[7], (V, RANK), 1.0, 6.0, ((0, 32),)),
        "proj_ffn": scatter_about(key_of[8], (FF, RANK), FF ** -0.5, 0.046875, ((0, 32),)),
        "proj_down": scatter_about(key_of[9], (D, RANK), 1.0, 6.0),
        "store": scatter_about(key_of[10], (NSTORE, F), F ** -0.5, 0.0625, ((0, 8), (1, 32))),
    }


epsilon = 1e-05
highest = lax.Precision.HIGHEST

def reference(hidden_in, norm_gain, head_weight, ffn_act, labels, lengths, proj_hidden, proj_vocab, proj_ffn, proj_down, store):
    token_count, model_width = hidden_in.shape
    query_count = lengths.shape[0]
    seq_span = token_count // query_count
    rank_size = proj_hidden.shape[1]
    vocab_size = head_weight.shape[1]
    wide_hidden = hidden_in.astype(jnp.float32)
    inverse = lax.rsqrt(lax.optimization_barrier(jnp.mean(wide_hidden * wide_hidden, axis=1, keepdims=True)) + epsilon)
    unit_hidden = wide_hidden * inverse
    normed = (norm_gain * unit_hidden).astype(jnp.bfloat16)
    positions = jnp.arange(token_count, dtype=jnp.int32) % seq_span
    valid = positions < jnp.repeat(lengths, seq_span)
    vocab_ids = jnp.arange(vocab_size, dtype=jnp.int32)[None, :]
    gained_down = norm_gain[:, None] * proj_down.astype(jnp.float32)

    def head_block(bundle):
        block_normed, block_labels, block_valid = bundle
        logits = jnp.dot(block_normed, head_weight, preferred_element_type=jnp.float32)
        peak = lax.optimization_barrier(jnp.max(logits, axis=1, keepdims=True))
        exponent = jnp.exp(logits - peak)
        probs = exponent / lax.optimization_barrier(jnp.sum(exponent, axis=1, keepdims=True))
        onehot = (block_labels[:, None] == vocab_ids).astype(jnp.float32)
        grads = jnp.where(block_valid[:, None], probs - onehot, 0.0).astype(jnp.bfloat16)
        back = lax.dot_general(grads, head_weight, (((1,), (1,)), ((), ())), preferred_element_type=jnp.float32)
        down_sum = jnp.dot(back, gained_down, precision=highest)
        label_dot = lax.optimization_barrier(jnp.sum(grads.astype(jnp.float32) * logits, axis=1))
        head_side = jnp.dot(grads, proj_vocab, preferred_element_type=jnp.float32)
        return (head_side, down_sum, label_dot)
    block_rows = token_count // N_GRP
    head_side, down_sum, label_dot = lax.map(head_block, (normed.reshape(N_GRP, block_rows, model_width), labels.reshape(N_GRP, block_rows), valid.reshape(N_GRP, block_rows)))
    head_side = head_side.reshape(token_count, rank_size)
    down_sum = down_sum.reshape(token_count, rank_size)
    label_dot = label_dot.reshape(token_count)
    hidden_side = jnp.dot(normed, proj_hidden, preferred_element_type=jnp.float32)
    ffn_side = jnp.dot(ffn_act, proj_ffn, preferred_element_type=jnp.float32)
    unit_down = jnp.dot(unit_hidden, proj_down.astype(jnp.float32), precision=highest)
    down_side = inverse * (down_sum - (label_dot / model_width)[:, None] * unit_down)
    shaped = (query_count, seq_span, rank_size)
    first_outer = jnp.einsum('spa,spb->sab', hidden_side.reshape(shaped), head_side.reshape(shaped))
    second_outer = jnp.einsum('spa,spb->sab', ffn_side.reshape(shaped), down_side.reshape(shaped))
    queries = jnp.concatenate([first_outer.reshape(query_count, -1), second_outer.reshape(query_count, -1)], axis=1).astype(jnp.bfloat16)
    return lax.dot_general(queries, store, (((1,), (1,)), ((), ())), preferred_element_type=jnp.float32)
```

```python
import jax
import jax.numpy as jnp
from jax import lax
from jax.experimental import pallas as pl
from jax.experimental.pallas import tpu as pltpu
from jax.sharding import PartitionSpec as P

epsilon = 1e-05
highest = lax.Precision.HIGHEST
f32 = jnp.float32
bf16 = jnp.bfloat16
by_last = (((1,), (1,)), ((), ()))


def vmem(count):
    return [pl.BlockSpec(memory_space=pltpu.VMEM)] * count


def traded(value, axis):
    return lax.all_to_all(value, axis, split_axis=0, concat_axis=0, tiled=True)


def sent_to_all(value, axis):
    return traded(jnp.broadcast_to(value, (lax.axis_size(axis), *value.shape)), axis)


def ring_gather(block, place, count, move):
    out = jnp.zeros((count, *block.shape), block.dtype)
    out = lax.dynamic_update_index_in_dim(out, block, place, 0)
    for shift in range(1, count):
        came = lax.ppermute(block, "tp", [(i, move(i, shift)) for i in range(lax.axis_size("tp"))])
        out = lax.dynamic_update_index_in_dim(out, came, (place - shift) % count, 0)
    return out


def soft_kernel(info, y_ref, vocab_ref, label_ref, out_ref):
    tokens, rank = label_ref.shape[0], vocab_ref.shape[0]
    columns = y_ref.shape[1]
    spot = lax.broadcasted_iota(jnp.int32, (1, columns), 1)
    counted = spot >= info[1]
    logits = y_ref[:tokens]
    peak = jnp.max(jnp.where(counted, logits, -jnp.inf), axis=1, keepdims=True)
    grown = jnp.where(counted, jnp.exp(jnp.minimum(logits - peak, 0.0)), 0.0)
    total = jnp.sum(grown, axis=1, keepdims=True)
    rounded = grown.astype(bf16)
    hit = counted & (label_ref[...] == spot + info[0])
    dot_all = jnp.sum(rounded.astype(f32) * logits, axis=1, keepdims=True)
    dot_hit = jnp.sum(jnp.where(hit, logits, 0.0), axis=1, keepdims=True)
    fold = y_ref[tokens : tokens + rank] + y_ref[tokens + rank : tokens + 2 * rank]
    fold_high = fold.astype(bf16)
    fold_low = (fold - fold_high.astype(f32)).astype(bf16)
    right = jnp.concatenate([vocab_ref[...], fold_high, fold_low, fold_low], axis=0)
    soft = lax.dot_general(rounded, right, by_last, preferred_element_type=f32)
    mark = lax.dot_general(
        hit.astype(f32).astype(bf16), right, by_last, preferred_element_type=f32
    )
    keep = lax.broadcasted_iota(jnp.int32, (1, 2 * rank), 1) >= rank
    out_ref[:, 0 : 2 * rank] = soft[:, : 2 * rank] + jnp.where(keep, soft[:, 2 * rank :], 0.0)
    out_ref[:, 2 * rank : 4 * rank] = mark[:, : 2 * rank] + jnp.where(keep, mark[:, 2 * rank :], 0.0)
    lane = lax.broadcasted_iota(jnp.int32, (tokens, 128), 1)
    stats = jnp.where(lane == 0, peak, jnp.where(lane == 1, total, jnp.where(lane == 2, dot_all, dot_hit)))
    out_ref[:, 4 * rank :] = stats


def merged(x):
    stats = x[:, :, 256:]
    peaks = stats[:, :, 0:1]
    peak = jnp.max(peaks, axis=0)
    weight = jnp.exp(peaks - peak)
    soft = jnp.sum(x[:, :, :128] * weight, axis=0)
    mark = jnp.sum(x[:, :, 128:256], axis=0)
    lane = lax.broadcasted_iota(jnp.int32, stats.shape[1:], 1)
    scaled = jnp.sum(stats * weight, axis=0)
    plain = jnp.sum(stats, axis=0)
    kept = jnp.where(lane == 0, peak, jnp.where(lane < 3, scaled, plain))
    return soft, mark, kept


def first_merge_kernel(x_ref, out_ref):
    soft, mark, kept = merged(x_ref[...])
    for copy in range(out_ref.shape[0]):
        out_ref[copy, :, :128] = soft
        out_ref[copy, :, 128:256] = mark
        out_ref[copy, :, 256:] = kept


def last_merge_kernel(x_ref, side_ref, unit_down_ref, out_ref, *, width):
    soft, mark, kept = merged(x_ref[...])
    total, dot_all, dot_hit = kept[:, 1:2], kept[:, 2:3], kept[:, 3:4]
    both = soft / total - mark
    label_dot = dot_all / total - dot_hit
    inverse, valid = side_ref[:, 0:1], side_ref[:, 1:2] > 0.0
    head_side = jnp.where(valid, both[:, :64], 0.0)
    down_side = inverse * (both[:, 64:] - (label_dot / width) * unit_down_ref[...])
    down_side = jnp.where(valid, down_side, 0.0)
    half = out_ref.shape[0] // 2
    for copy in range(half):
        out_ref[copy] = head_side
        out_ref[half + copy] = down_side


def score_kernel(left_ref, right_ref, store_ref, out_ref, query_ref):
    @pl.when(pl.program_id(0) == 0)
    def _():
        right = right_ref[...]
        parts = []
        for a in range(left_ref.shape[1]):
            product = left_ref[:, a : a + 1] * right
            parts.append(jnp.sum(product.reshape(-1, 8, right.shape[1]), axis=1))
        query_ref[...] = jnp.concatenate(parts, axis=1).astype(bf16)

    out_ref[...] = lax.dot_general(
        query_ref[...], store_ref[...], by_last, preferred_element_type=f32
    ).astype(out_ref.dtype)


def per_device(
    hidden_in,
    norm_gain,
    head_weight,
    ffn_act,
    labels,
    lengths,
    proj_hidden,
    proj_vocab,
    proj_ffn,
    proj_down,
    store,
):
    here, width = hidden_in.shape
    rows_owned, vocab_owned = head_weight.shape
    rank = proj_hidden.shape[1]
    groups, lanes = lax.axis_size("grp"), lax.axis_size("tp")
    tokens = here * groups
    seq_span = here // lengths.shape[0]
    z, j = lax.axis_index("grp"), lax.axis_index("tp")

    block = -(-vocab_owned // (8 * groups)) * 8
    turned = head_weight.T

    def first_of(group):
        return jnp.minimum(block * group, vocab_owned - block)

    shifts = (4, 3, 5, 2, 6, 1, 7)
    came = {}
    for s in shifts:
        cut = lax.dynamic_slice_in_dim(turned, first_of((z + s) % groups), block, 0)
        came[s] = lax.ppermute(cut, "grp", [(i, (i + s) % groups) for i in range(groups)])
    came[0] = lax.dynamic_slice_in_dim(turned, first_of(z), block, 0)
    start = first_of(z)
    skipped = block * z - start

    part = width // lanes
    share = lax.dynamic_slice_in_dim(hidden_in, j * part, part, 1)
    column = sent_to_all(share, "grp").reshape(tokens, part)
    y_at, x_at, core_at = j // 8, (j // 2) % 4, j % 2
    gathered = ring_gather(column, x_at, 4, lambda i, s: i // 8 * 8 + (i % 8 + 2 * s) % 8)
    gathered = ring_gather(gathered, y_at, 4, lambda i, s: (i + 8 * s) % 32)
    gathered = ring_gather(gathered, core_at, 2, lambda i, s: i ^ 1)
    hidden = gathered.transpose(3, 1, 2, 0, 4).reshape(tokens, width)
    wide = hidden.astype(f32)
    inverse = lax.rsqrt(jnp.mean(wide * wide, axis=1, keepdims=True) + epsilon)
    normed = (norm_gain * (wide * inverse)).astype(bf16)

    gained_down = norm_gain[None, :] * proj_down.T.astype(f32)
    down_high = gained_down.astype(bf16)
    down_low = (gained_down - down_high.astype(f32)).astype(bf16)
    lhs = jnp.concatenate([normed, down_high, down_low], axis=0)
    sums = None
    for s in (0, *shifts):
        depth = lax.dynamic_slice_in_dim(lhs, ((z - s) % groups) * rows_owned, rows_owned, 1)
        term = lax.dot_general(depth, came[s], by_last, preferred_element_type=f32)
        sums = term if sums is None else sums + term

    ints = jnp.concatenate([labels, lengths])
    ints = sent_to_all(ints[None], "grp").reshape(groups, -1)
    all_labels = ints[:, :here].reshape(tokens, 1)
    all_lengths = ints[:, here:].reshape(-1)
    mine = tokens // lanes
    spot = j * mine + lax.broadcasted_iota(jnp.int32, (mine, 1), 0)
    own_length = lax.dynamic_slice_in_dim(all_lengths, j * (mine // seq_span), mine // seq_span, 0)
    valid = spot % seq_span < jnp.repeat(own_length, seq_span)[:, None]
    own_hidden = lax.dynamic_slice_in_dim(wide, j * mine, mine, 0)
    own_inverse = lax.dynamic_slice_in_dim(inverse, j * mine, mine, 0)
    unit_down = jnp.dot(own_hidden * own_inverse, proj_down.astype(f32), precision=highest)
    side = jnp.concatenate([own_inverse, valid.astype(f32), jnp.zeros((mine, 126), f32)], axis=1)

    per = store.shape[1] // rank
    half = lanes // 2
    hidden_side = jnp.dot(normed, proj_hidden, preferred_element_type=f32)
    left_head = lax.dynamic_slice_in_dim(hidden_side, (j % half) * per, per, 1)
    ffn = jnp.dot(ffn_act, proj_ffn, preferred_element_type=f32)
    few = here // lanes
    ffn = traded(ffn.reshape(lanes, 1, few * rank), "tp").sum(axis=0)
    ffn = sent_to_all(ffn, "grp").reshape(groups * few, half, per)
    ffn = ffn.transpose(1, 0, 2).reshape(half, 1, groups * few * per)
    ffn = traded(jnp.concatenate([ffn, ffn], axis=0), "tp")
    ffn = ffn.reshape(lanes, groups, few, per).transpose(1, 0, 2, 3).reshape(tokens, per)
    left = jnp.where(j < half, left_head, ffn)

    vocab_turned = lax.dynamic_slice_in_dim(proj_vocab, start, block, 0).T
    info = jnp.stack([j * vocab_owned + start, skipped]).astype(jnp.int32)
    packed = pl.pallas_call(
        soft_kernel,
        out_shape=jax.ShapeDtypeStruct((tokens, 4 * rank + 128), f32),
        in_specs=[pl.BlockSpec(memory_space=pltpu.SMEM), *vmem(3)],
        out_specs=pl.BlockSpec(memory_space=pltpu.VMEM),
    )(info, sums, vocab_turned, all_labels)
    wide_row = packed.shape[1]
    packed = traded(packed.reshape(lanes, mine, wide_row), "tp")
    packed = pl.pallas_call(
        first_merge_kernel,
        out_shape=jax.ShapeDtypeStruct((groups, mine, wide_row), f32),
        in_specs=vmem(1),
        out_specs=pl.BlockSpec(memory_space=pltpu.VMEM),
    )(packed)
    packed = traded(packed, "grp")
    right = pl.pallas_call(
        lambda *refs: last_merge_kernel(*refs, width=width),
        out_shape=jax.ShapeDtypeStruct((lanes, mine, rank), f32),
        in_specs=vmem(3),
        out_specs=pl.BlockSpec(memory_space=pltpu.VMEM),
    )(packed, side, unit_down)
    right = traded(right, "tp").reshape(tokens, rank)

    stored, features = store.shape
    step = 1024
    queries = tokens // seq_span
    partial = pl.pallas_call(
        score_kernel,
        grid=(stored // step,),
        out_shape=jax.ShapeDtypeStruct((queries, stored), bf16),
        in_specs=[
            pl.BlockSpec((tokens, per), lambda i: (0, 0)),
            pl.BlockSpec((tokens, rank), lambda i: (0, 0)),
            pl.BlockSpec((step, features), lambda i: (i, 0)),
        ],
        out_specs=pl.BlockSpec((queries, step), lambda i: (0, i)),
        scratch_shapes=[pltpu.VMEM((queries, features), bf16)],
    )(left, right, store)
    partial = traded(partial.reshape(lanes, queries // lanes, stored), "tp")
    return jnp.sum(partial.astype(f32), axis=0)


def solution(mesh):
    return jax.shard_map(
        per_device,
        mesh=mesh,
        in_specs=(
            P("grp", None),
            P(),
            P("grp", "tp"),
            P("grp", "tp"),
            P("grp"),
            P("grp"),
            P(),
            P("tp", None),
            P("tp", None),
            P(),
            P("grp", "tp"),
        ),
        out_specs=P("tp", "grp"),
        check_vma=False,
    )
```

```python
import jax
import jax.numpy as jnp
from jax import lax
from jax.experimental import pallas as pl
from jax.experimental.pallas import tpu as pltpu
from jax.sharding import PartitionSpec as P


epsilon = 1e-05
f32 = jnp.float32
bf16 = jnp.bfloat16
by_last = (((1,), (1,)), ((), ()))

early_shifts = (1, 7)
late_shifts = (4, 3, 5, 2, 6)


small = pltpu.CompilerParams(vmem_limit_bytes=16 * 1024 * 1024)


def vmem(count):
    return [pl.BlockSpec(memory_space=pltpu.VMEM)] * count


def traded(value, axis, groups=None):
    return lax.all_to_all(
        value, axis, split_axis=0, concat_axis=0, tiled=True, axis_index_groups=groups
    )


def norm_kernel(info, gain_ref, down_ref, hidden_proj_ref, *refs, width):
    pieces, (lhs_ref, side_ref, own_ref) = refs[:-3], refs[-3:]
    xs, tokens, lane = pieces[0].shape
    rank = down_ref.shape[0]
    mine = side_ref.shape[0]
    rows = 64
    half = len(pieces) // 2
    places = []
    for n in range(len(pieces)):
        y = lax.rem(info[0] + half - n % half, half)
        core = info[1] if n < half else 1 - info[1]
        for x in range(xs):
            places.append((n, x, pl.multiple_of(((y * xs + x) * 2 + core) * lane, lane)))

    @pl.loop(0, tokens // rows)
    def _(i):
        at = pl.ds(pl.multiple_of(i * rows, rows), rows)
        squares = jnp.zeros((rows, lane), f32)
        for n, x, _ in places:
            value = pieces[n][x, at, :].astype(f32)
            squares += value * value
        mean = jnp.sum(squares, axis=1, keepdims=True) / width
        inverse = jnp.broadcast_to(lax.rsqrt(mean + epsilon), (rows, lane))
        for n, x, place in places:
            value = pieces[n][x, at, :].astype(f32)
            lhs_ref[at, pl.ds(place, lane)] = (gain_ref[:, pl.ds(place, lane)] * (value * inverse)).astype(bf16)

    gained = gain_ref[...] * down_ref[...].astype(f32)
    high = gained.astype(bf16)
    lhs_ref[tokens : tokens + rank] = high
    lhs_ref[tokens + rank :] = (gained - high.astype(f32)).astype(bf16)
    own = pl.ds(pl.multiple_of(info[2], mine), mine)
    squares = jnp.zeros((mine, lane), f32)
    for n, x, place in places:
        value = pieces[n][x, own, :]
        own_ref[:, pl.ds(place, lane)] = value
        squares += value.astype(f32) * value.astype(f32)
    inverse = lax.rsqrt(jnp.sum(squares, axis=1, keepdims=True) / width + epsilon)
    unit_down = inverse * lax.dot_general(own_ref[...], down_ref[...], by_last, preferred_element_type=f32)
    hidden_side = lax.dot_general(
        lhs_ref[own, :], hidden_proj_ref[...], by_last, preferred_element_type=f32
    )
    side_ref[:, :rank] = unit_down
    side_ref[:, rank : 2 * rank] = hidden_side
    side_ref[:, 2 * rank :] = jnp.broadcast_to(inverse, (mine, side_ref.shape[1] - 2 * rank))


def soft_kernel(
    info, sums_ref, lhs_ref, first_ref, last_ref, vocab_ref, label_ref, ffn_ref, keep_ref, send_ref, out_ref
):
    tokens, rank = label_ref.shape[0], vocab_ref.shape[0]
    columns, depth = last_ref.shape

    def finished(first, count):
        total = sums_ref[first : first + count]
        for n, ref in enumerate((first_ref, last_ref)):
            at = pl.ds(pl.multiple_of(info[4 + n], depth), depth)
            total += lax.dot_general(
                lhs_ref[first : first + count, at], ref[...], by_last, preferred_element_type=f32
            )
        return total

    fold = finished(tokens, 2 * rank)
    fold = fold[:rank] + fold[rank:]
    fold_high = fold.astype(bf16)
    fold_low = (fold - fold_high.astype(f32)).astype(bf16)
    right = jnp.concatenate([vocab_ref[...], fold_high, fold_low, fold_low], axis=0)
    keep = lax.broadcasted_iota(jnp.int32, (1, 2 * rank), 1) >= rank
    spot = lax.broadcasted_iota(jnp.int32, (1, columns), 1)
    counted = spot >= info[1]
    count = 128
    lane = lax.broadcasted_iota(jnp.int32, (count, 2 * rank), 1)
    for first in range(0, tokens, count):
        rows = slice(first, first + count)
        logits = finished(first, count)
        peak = jnp.max(jnp.where(counted, logits, -jnp.inf), axis=1, keepdims=True)
        grown = jnp.where(counted, jnp.exp(jnp.minimum(logits - peak, 0.0)), 0.0)
        total = jnp.sum(grown, axis=1, keepdims=True)
        rounded = grown.astype(bf16)
        hit = counted & (label_ref[rows] == spot + info[0])
        dot_all = jnp.sum(rounded.astype(f32) * logits, axis=1, keepdims=True)
        dot_hit = jnp.sum(jnp.where(hit, logits, 0.0), axis=1, keepdims=True)
        soft = lax.dot_general(rounded, right, by_last, preferred_element_type=f32)
        mark = lax.dot_general(hit.astype(f32).astype(bf16), right, by_last, preferred_element_type=f32)
        out_ref[rows, : 2 * rank] = soft[:, : 2 * rank] + jnp.where(keep, soft[:, 2 * rank :], 0.0)
        out_ref[rows, 2 * rank : 4 * rank] = mark[:, : 2 * rank] + jnp.where(keep, mark[:, 2 * rank :], 0.0)
        stats = jnp.where(lane == 0, peak, jnp.where(lane == 1, total, jnp.where(lane == 2, dot_all, dot_hit)))
        out_ref[rows, 4 * rank :] = jnp.where(lane < 4, stats, 0.0)
    here = ffn_ref.shape[0]
    own = pl.ds(pl.multiple_of(info[2], here), here)
    lane = lax.broadcasted_iota(jnp.int32, (here, 2 * rank), 1)
    out_ref[own, 4 * rank :] = jnp.where(lane < rank, out_ref[own, 4 * rank :], ffn_ref[...])
    mine = keep_ref.shape[1]
    for core in range(2):

        @pl.when(info[3] == core)
        def _():
            for pair in range(keep_ref.shape[0]):
                first, second = 2 * pair + core, 2 * pair + 1 - core
                keep_ref[pair] = out_ref[mine * first : mine * (first + 1)]
                send_ref[pair] = out_ref[mine * second : mine * (second + 1)]


def merged(x):
    stats = x[:, :, 256:]
    peaks = stats[:, :, 0:1]
    peak = jnp.max(peaks, axis=0)
    weight = jnp.exp(peaks - peak)
    soft = jnp.sum(x[:, :, :128] * weight, axis=0)
    mark = jnp.sum(x[:, :, 128:256], axis=0)
    lane = lax.broadcasted_iota(jnp.int32, stats.shape[1:], 1)
    scaled = jnp.sum(stats * weight, axis=0)
    plain = jnp.sum(stats, axis=0)
    kept = jnp.where(lane == 0, peak, jnp.where(lane < 3, scaled, plain))
    return soft, mark, kept


def pair_merge_kernel(keep_ref, came_ref, out_ref):
    for n in range(out_ref.shape[0]):
        soft, mark, kept = merged(jnp.stack([keep_ref[n], came_ref[n]]))
        out_ref[n, :, :128] = soft
        out_ref[n, :, 128:256] = mark
        out_ref[n, :, 256:] = kept


def first_merge_kernel(x_ref, out_ref):
    soft, mark, kept = merged(x_ref[...])
    for copy in range(out_ref.shape[0]):
        out_ref[copy, :, :128] = soft
        out_ref[copy, :, 128:256] = mark
        out_ref[copy, :, 256:] = kept


def last_merge_kernel(x_ref, side_ref, valid_ref, out_ref, *, width):
    soft, mark, kept = merged(x_ref[...])
    total, dot_all, dot_hit = kept[:, 1:2], kept[:, 2:3], kept[:, 3:4]
    both = soft / total - mark
    label_dot = dot_all / total - dot_hit
    rank = both.shape[1] // 2
    inverse, valid = side_ref[:, 2 * rank : 2 * rank + 1], valid_ref[...] > 0
    down_side = inverse * (both[:, rank:] - (label_dot / width) * side_ref[:, :rank])
    head_side = jnp.where(valid, both[:, :rank], 0.0)
    down_side = jnp.where(valid, down_side, 0.0)
    first = jnp.concatenate([head_side, side_ref[:, rank : 2 * rank]], axis=1).astype(bf16)
    second = jnp.concatenate([down_side, kept[:, rank:]], axis=1).astype(bf16)
    half = out_ref.shape[0] // 2
    for copy in range(half):
        out_ref[copy] = first
        out_ref[half + copy] = second


def query_kernel(info, sides_ref, out_ref, *, span):
    rank = sides_ref.shape[1] // 2
    sides = sides_ref[...]
    features = out_ref.shape[1]
    column = lax.broadcasted_iota(jnp.int32, (2 * rank, features), 0)
    wanted = rank + info[0] + lax.broadcasted_iota(jnp.int32, (2 * rank, features), 1) // rank
    chosen = (column == wanted).astype(f32).astype(bf16)
    left = jnp.dot(sides, chosen, preferred_element_type=f32)
    right = sides[:, :rank].astype(f32)
    product = left * jnp.concatenate([right] * (features // rank), axis=1)
    query = jnp.sum(product.reshape(-1, span, features), axis=1).astype(bf16)
    count = query.shape[0]
    spot = lax.broadcasted_iota(jnp.int32, (count, count), 0)
    source = lax.broadcasted_iota(jnp.int32, (count, count), 1)
    half, each = count // 2, info[1]
    far = spot // half
    near = spot - far * half
    core = info[2] + far - 2 * info[2] * far
    wanted = (2 * (near // each) + core) * each + lax.rem(near, each)
    order = (source == wanted).astype(f32).astype(bf16)
    out_ref[...] = jnp.dot(order, query, preferred_element_type=f32).astype(bf16)


def per_device(
    hidden_in,
    norm_gain,
    head_weight,
    ffn_act,
    labels,
    lengths,
    proj_hidden,
    proj_vocab,
    proj_ffn,
    proj_down,
    store,
):
    here, width = hidden_in.shape
    rows_owned, vocab_owned = head_weight.shape
    rank = proj_hidden.shape[1]
    groups, lanes = lax.axis_size("grp"), lax.axis_size("tp")
    tokens = here * groups
    seq_span = here // lengths.shape[0]
    z, j = lax.axis_index("grp"), lax.axis_index("tp")

    block = -(-vocab_owned // (8 * groups)) * 8
    turned = head_weight.T

    def first_of(group):
        return jnp.minimum(block * group, vocab_owned - block)

    start = first_of(z)
    skipped = block * z - start

    part = width // lanes
    digits = [labels % 128, labels // 128 % 128, labels // 16384, lengths]
    digits = jnp.concatenate(digits).astype(bf16)
    digits = jnp.pad(digits, (0, 16 * part - digits.shape[0])).reshape(16, part)
    share = lax.dynamic_slice_in_dim(hidden_in, j * part, part, 1)
    share = jnp.concatenate([share, digits], axis=0)

    came = {}

    def head_moves(source, shifts):
        for s in shifts:
            cut = lax.dynamic_slice_in_dim(source, first_of((z + s) % groups), block, 0)
            came[s] = lax.ppermute(cut, "grp", [(i, (i + s) % groups) for i in range(groups)])

    head_moves(turned, early_shifts)
    later, share = lax.optimization_barrier((turned, share))
    head_moves(later, late_shifts)
    came[0] = lax.dynamic_slice_in_dim(later, start, block, 0)
    column = jnp.zeros((groups, here, part), bf16)
    ints = jnp.zeros((groups, 2, part), bf16)
    for s in range(groups):
        got = lax.ppermute(share, "grp", [(i, (i + s) % groups) for i in range(groups)]) if s else share
        column = lax.dynamic_update_index_in_dim(column, got[:here], (z - s) % groups, 0)
        ints = lax.dynamic_update_index_in_dim(ints, got[here : here + 2], (z - s) % groups, 0)
    column = column.reshape(tokens, part)
    y_at, x_at, core_at = j // 8, (j // 2) % 4, j % 2

    def moved(value, move):
        return lax.ppermute(value, "tp", [(i, move(i)) for i in range(lanes)])

    row = jnp.zeros((4, tokens, part), bf16)
    for s in range(4):
        came_x = moved(column, lambda i: i // 8 * 8 + (i % 8 + 2 * s) % 8) if s else column
        row = lax.dynamic_update_index_in_dim(row, came_x, (x_at - s) % 4, 0)
    pieces = [moved(row, lambda i: (i + 8 * s) % 32) if s else row for s in range(4)]
    pieces += [moved(piece, lambda i: i ^ 1) for piece in pieces]

    mine = tokens // lanes
    of_one_core = [[2 * i + core for i in range(lanes // 2)] for core in range(2)]
    in_smem = pl.BlockSpec(memory_space=pltpu.SMEM)
    in_vmem = pl.BlockSpec(memory_space=pltpu.VMEM)
    lhs, side = pl.pallas_call(
        lambda *refs: norm_kernel(*refs, width=width),
        out_shape=(
            jax.ShapeDtypeStruct((tokens + 2 * rank, width), bf16),
            jax.ShapeDtypeStruct((mine, 4 * rank), f32),
        ),
        in_specs=[in_smem, *vmem(3 + len(pieces))],
        out_specs=(in_vmem, in_vmem),
        scratch_shapes=[pltpu.VMEM((mine, width), bf16)],
        compiler_params=small,
    )(
        jnp.stack([y_at, core_at, j * mine]).astype(jnp.int32),
        norm_gain[None, :],
        proj_down.T,
        proj_hidden.T,
        *pieces,
    )

    ints = ints.astype(jnp.int32).reshape(groups, 2 * part)
    all_labels = ints[:, :here] + 128 * ints[:, here : 2 * here] + 16384 * ints[:, 2 * here : 3 * here]
    all_labels = all_labels.reshape(tokens, 1)
    all_lengths = ints[:, 3 * here : 3 * here + lengths.shape[0]].reshape(-1)
    spot = j * mine + lax.broadcasted_iota(jnp.int32, (mine, 1), 0)
    own_length = lax.dynamic_slice_in_dim(all_lengths, j * (mine // seq_span), mine // seq_span, 0)
    valid = (spot % seq_span < jnp.repeat(own_length, seq_span)[:, None]).astype(jnp.int32)
    ffn = jnp.dot(ffn_act, proj_ffn, preferred_element_type=f32)
    ffn = jnp.concatenate([jnp.zeros_like(ffn), ffn], axis=1)
    vocab_turned = lax.dynamic_slice_in_dim(proj_vocab, start, block, 0).T

    sums = None
    shifts = (0, *early_shifts, *late_shifts)
    for s in shifts[:-2]:
        depth = lax.dynamic_slice_in_dim(lhs, ((z - s) % groups) * rows_owned, rows_owned, 1)
        term = lax.dot_general(depth, came[s], by_last, preferred_element_type=f32)
        sums = term if sums is None else sums + term
    last = shifts[-2:]
    info = [j * vocab_owned + start, skipped, z * here, core_at]
    info = jnp.stack([*info, *(((z - s) % groups) * rows_owned for s in last)]).astype(jnp.int32)
    by_core = (lanes // 2, mine, 6 * rank)
    keep, send = pl.pallas_call(
        soft_kernel,
        out_shape=(jax.ShapeDtypeStruct(by_core, f32), jax.ShapeDtypeStruct(by_core, f32)),
        in_specs=[in_smem, *vmem(7)],
        out_specs=(in_vmem, in_vmem),
        scratch_shapes=[pltpu.VMEM((tokens, 6 * rank), f32)],
        compiler_params=small,
    )(info, sums, lhs, came[last[0]], came[last[1]], vocab_turned, all_labels, ffn)
    packed = pl.pallas_call(
        pair_merge_kernel,
        out_shape=jax.ShapeDtypeStruct(by_core, f32),
        in_specs=vmem(2),
        out_specs=in_vmem,
        compiler_params=small,
    )(keep, moved(send, lambda i: i ^ 1))
    packed = traded(packed, "tp", of_one_core)
    packed = pl.pallas_call(
        first_merge_kernel,
        out_shape=jax.ShapeDtypeStruct((groups, mine, 6 * rank), f32),
        in_specs=vmem(1),
        out_specs=in_vmem,
        compiler_params=small,
    )(packed)
    packed = traded(packed, "grp")
    sides = pl.pallas_call(
        lambda *refs: last_merge_kernel(*refs, width=width),
        out_shape=jax.ShapeDtypeStruct((lanes, mine, 2 * rank), bf16),
        in_specs=vmem(3),
        out_specs=in_vmem,
        compiler_params=small,
    )(packed, side, valid)
    sides = traded(sides, "tp").reshape(tokens, 2 * rank)

    stored, features = store.shape
    queries = tokens // seq_span
    per = features // rank
    query = pl.pallas_call(
        lambda *refs: query_kernel(*refs, span=seq_span),
        out_shape=jax.ShapeDtypeStruct((queries, features), bf16),
        in_specs=[in_smem, *vmem(1)],
        out_specs=in_vmem,
        compiler_params=small,
    )(jnp.stack([j % (lanes // 2) * per, queries // lanes, core_at]).astype(jnp.int32), sides)
    partial = lax.dot_general(query, store, by_last, preferred_element_type=f32)
    half = queries // 2
    other = moved(partial[half:].astype(bf16), lambda i: i ^ 1)
    partial = (partial[:half] + other.astype(f32)).astype(bf16)
    partial = traded(partial.reshape(lanes // 2, queries // lanes, stored), "tp", of_one_core)
    return jnp.sum(partial.astype(f32), axis=0)


def solution(mesh):
    return jax.shard_map(
        per_device,
        mesh=mesh,
        in_specs=(
            P("grp", None),
            P(),
            P("grp", "tp"),
            P("grp", "tp"),
            P("grp"),
            P("grp"),
            P(),
            P("tp", None),
            P("tp", None),
            P(),
            P("grp", "tp"),
        ),
        out_specs=P("tp", "grp"),
        check_vma=False,
    )
```

```python
import jax
import jax.numpy as jnp
from jax import lax
from jax.experimental import pallas as pl
from jax.experimental.pallas import tpu as pltpu
from jax.sharding import PartitionSpec as P


epsilon = 1e-05
f32 = jnp.float32
bf16 = jnp.bfloat16
by_last = (((1,), (1,)), ((), ()))

early_shifts = (1, 7)
late_shifts = (4, 3, 5, 2, 6)


small = pltpu.CompilerParams(vmem_limit_bytes=16 * 1024 * 1024)


def vmem(count):
    return [pl.BlockSpec(memory_space=pltpu.VMEM)] * count


def traded(value, axis, groups=None):
    return lax.all_to_all(
        value, axis, split_axis=0, concat_axis=0, tiled=True, axis_index_groups=groups
    )


def norm_kernel(info, gain_ref, down_ref, hidden_proj_ref, *refs, width):
    pieces, (lhs_ref, side_ref, own_ref) = refs[:-3], refs[-3:]
    xs, tokens, lane = pieces[0].shape
    rank = down_ref.shape[0]
    mine = side_ref.shape[0]
    rows = 64
    half = len(pieces) // 2
    places = []
    for n in range(len(pieces)):
        y = lax.rem(info[0] + half - n % half, half)
        core = info[1] if n < half else 1 - info[1]
        for x in range(xs):
            places.append((n, x, pl.multiple_of(((y * xs + x) * 2 + core) * lane, lane)))

    @pl.loop(0, tokens // rows)
    def _(i):
        at = pl.ds(pl.multiple_of(i * rows, rows), rows)
        squares = jnp.zeros((rows, lane), f32)
        for n, x, _ in places:
            value = pieces[n][x, at, :].astype(f32)
            squares += value * value
        mean = jnp.sum(squares, axis=1, keepdims=True) / width
        inverse = jnp.broadcast_to(lax.rsqrt(mean + epsilon), (rows, lane))
        for n, x, place in places:
            value = pieces[n][x, at, :].astype(f32)
            lhs_ref[at, pl.ds(place, lane)] = (gain_ref[:, pl.ds(place, lane)] * (value * inverse)).astype(bf16)

    gained = gain_ref[...] * down_ref[...].astype(f32)
    high = gained.astype(bf16)
    lhs_ref[tokens : tokens + rank] = high
    lhs_ref[tokens + rank :] = (gained - high.astype(f32)).astype(bf16)
    own = pl.ds(pl.multiple_of(info[2], mine), mine)
    squares = jnp.zeros((mine, lane), f32)
    for n, x, place in places:
        value = pieces[n][x, own, :]
        own_ref[:, pl.ds(place, lane)] = value
        squares += value.astype(f32) * value.astype(f32)
    inverse = lax.rsqrt(jnp.sum(squares, axis=1, keepdims=True) / width + epsilon)
    unit_down = inverse * lax.dot_general(own_ref[...], down_ref[...], by_last, preferred_element_type=f32)
    hidden_side = lax.dot_general(
        lhs_ref[own, :], hidden_proj_ref[...], by_last, preferred_element_type=f32
    )
    side_ref[:, :rank] = unit_down
    side_ref[:, rank : 2 * rank] = hidden_side
    side_ref[:, 2 * rank :] = jnp.broadcast_to(inverse, (mine, side_ref.shape[1] - 2 * rank))


def soft_kernel(
    info, sums_ref, lhs_ref, first_ref, last_ref, vocab_ref, label_ref, ffn_ref, keep_ref, send_ref, out_ref
):
    tokens, rank = label_ref.shape[0], vocab_ref.shape[0]
    columns, depth = last_ref.shape

    def finished(first, count):
        total = sums_ref[first : first + count]
        for n, ref in enumerate((first_ref, last_ref)):
            at = pl.ds(pl.multiple_of(info[4 + n], depth), depth)
            total += lax.dot_general(
                lhs_ref[first : first + count, at], ref[...], by_last, preferred_element_type=f32
            )
        return total

    fold = finished(tokens, 2 * rank)
    fold = fold[:rank] + fold[rank:]
    fold_high = fold.astype(bf16)
    fold_low = (fold - fold_high.astype(f32)).astype(bf16)
    right = jnp.concatenate([vocab_ref[...], fold_high, fold_low, fold_low], axis=0)
    keep = lax.broadcasted_iota(jnp.int32, (1, 2 * rank), 1) >= rank
    spot = lax.broadcasted_iota(jnp.int32, (1, columns), 1)
    counted = spot >= info[1]
    count = 128
    lane = lax.broadcasted_iota(jnp.int32, (count, 2 * rank), 1)
    for first in range(0, tokens, count):
        rows = slice(first, first + count)
        logits = finished(first, count)
        peak = jnp.max(jnp.where(counted, logits, -jnp.inf), axis=1, keepdims=True)
        grown = jnp.where(counted, jnp.exp(jnp.minimum(logits - peak, 0.0)), 0.0)
        total = jnp.sum(grown, axis=1, keepdims=True)
        rounded = grown.astype(bf16)
        hit = counted & (label_ref[rows] == spot + info[0])
        dot_all = jnp.sum(rounded.astype(f32) * logits, axis=1, keepdims=True)
        dot_hit = jnp.sum(jnp.where(hit, logits, 0.0), axis=1, keepdims=True)
        soft = lax.dot_general(rounded, right, by_last, preferred_element_type=f32)
        mark = lax.dot_general(hit.astype(f32).astype(bf16), right, by_last, preferred_element_type=f32)
        out_ref[rows, : 2 * rank] = soft[:, : 2 * rank] + jnp.where(keep, soft[:, 2 * rank :], 0.0)
        out_ref[rows, 2 * rank : 4 * rank] = mark[:, : 2 * rank] + jnp.where(keep, mark[:, 2 * rank :], 0.0)
        stats = jnp.where(lane == 0, peak, jnp.where(lane == 1, total, jnp.where(lane == 2, dot_all, dot_hit)))
        out_ref[rows, 4 * rank :] = jnp.where(lane < 4, stats, 0.0)
    here = ffn_ref.shape[0]
    own = pl.ds(pl.multiple_of(info[2], here), here)
    lane = lax.broadcasted_iota(jnp.int32, (here, 2 * rank), 1)
    out_ref[own, 4 * rank :] = jnp.where(lane < rank, out_ref[own, 4 * rank :], ffn_ref[...])
    mine = keep_ref.shape[1]
    for core in range(2):

        @pl.when(info[3] == core)
        def _():
            for pair in range(keep_ref.shape[0]):
                first, second = 2 * pair + core, 2 * pair + 1 - core
                keep_ref[pair] = out_ref[mine * first : mine * (first + 1)]
                send_ref[pair] = out_ref[mine * second : mine * (second + 1)]


def merged(x):
    stats = x[:, :, 256:]
    peaks = stats[:, :, 0:1]
    peak = jnp.max(peaks, axis=0)
    weight = jnp.exp(peaks - peak)
    soft = jnp.sum(x[:, :, :128] * weight, axis=0)
    mark = jnp.sum(x[:, :, 128:256], axis=0)
    lane = lax.broadcasted_iota(jnp.int32, stats.shape[1:], 1)
    scaled = jnp.sum(stats * weight, axis=0)
    plain = jnp.sum(stats, axis=0)
    kept = jnp.where(lane == 0, peak, jnp.where(lane < 3, scaled, plain))
    return soft, mark, kept


def pair_merge_kernel(keep_ref, came_ref, out_ref):
    for n in range(out_ref.shape[0]):
        soft, mark, kept = merged(jnp.stack([keep_ref[n], came_ref[n]]))
        out_ref[n, :, :128] = soft
        out_ref[n, :, 128:256] = mark
        out_ref[n, :, 256:] = kept


def first_merge_kernel(x_ref, out_ref):
    soft, mark, kept = merged(x_ref[...])
    for copy in range(out_ref.shape[0]):
        out_ref[copy, :, :128] = soft
        out_ref[copy, :, 128:256] = mark
        out_ref[copy, :, 256:] = kept


def last_merge_kernel(x_ref, side_ref, valid_ref, out_ref, *, width):
    soft, mark, kept = merged(x_ref[...])
    total, dot_all, dot_hit = kept[:, 1:2], kept[:, 2:3], kept[:, 3:4]
    both = soft / total - mark
    label_dot = dot_all / total - dot_hit
    rank = both.shape[1] // 2
    inverse, valid = side_ref[:, 2 * rank : 2 * rank + 1], valid_ref[...] > 0
    down_side = inverse * (both[:, rank:] - (label_dot / width) * side_ref[:, :rank])
    head_side = jnp.where(valid, both[:, :rank], 0.0)
    down_side = jnp.where(valid, down_side, 0.0)
    first = jnp.concatenate([head_side, side_ref[:, rank : 2 * rank]], axis=1).astype(bf16)
    second = jnp.concatenate([down_side, kept[:, rank:]], axis=1).astype(bf16)
    half = out_ref.shape[0] // 2
    for copy in range(half):
        out_ref[copy] = first
        out_ref[half + copy] = second


def query_kernel(info, sides_ref, out_ref, *, span):
    rank = sides_ref.shape[1] // 2
    sides = sides_ref[...]
    features = out_ref.shape[1]
    column = lax.broadcasted_iota(jnp.int32, (2 * rank, features), 0)
    wanted = rank + info[0] + lax.broadcasted_iota(jnp.int32, (2 * rank, features), 1) // rank
    chosen = (column == wanted).astype(f32).astype(bf16)
    left = jnp.dot(sides, chosen, preferred_element_type=f32)
    right = sides[:, :rank].astype(f32)
    product = left * jnp.concatenate([right] * (features // rank), axis=1)
    query = jnp.sum(product.reshape(-1, span, features), axis=1).astype(bf16)
    count = query.shape[0]
    spot = lax.broadcasted_iota(jnp.int32, (count, count), 0)
    source = lax.broadcasted_iota(jnp.int32, (count, count), 1)
    half, each = count // 2, info[1]
    far = spot // half
    near = spot - far * half
    core = info[2] + far - 2 * info[2] * far
    wanted = (2 * (near // each) + core) * each + lax.rem(near, each)
    order = (source == wanted).astype(f32).astype(bf16)
    out_ref[...] = jnp.dot(order, query, preferred_element_type=f32).astype(bf16)


def per_device(
    hidden_in,
    norm_gain,
    head_weight,
    ffn_act,
    labels,
    lengths,
    proj_hidden,
    proj_vocab,
    proj_ffn,
    proj_down,
    store,
):
    here, width = hidden_in.shape
    rows_owned, vocab_owned = head_weight.shape
    rank = proj_hidden.shape[1]
    groups, lanes = lax.axis_size("grp"), lax.axis_size("tp")
    tokens = here * groups
    seq_span = here // lengths.shape[0]
    z, j = lax.axis_index("grp"), lax.axis_index("tp")

    block = -(-vocab_owned // (8 * groups)) * 8
    turned = head_weight.T

    def first_of(group):
        return jnp.minimum(block * group, vocab_owned - block)

    start = first_of(z)
    skipped = block * z - start

    part = width // lanes
    digits = [labels % 128, labels // 128 % 128, labels // 16384, lengths]
    digits = jnp.concatenate(digits).astype(bf16)
    digits = jnp.pad(digits, (0, 16 * part - digits.shape[0])).reshape(16, part)
    share = lax.dynamic_slice_in_dim(hidden_in, j * part, part, 1)
    share = jnp.concatenate([share, digits], axis=0)

    came = {}

    def head_moves(source, shifts):
        for s in shifts:
            cut = lax.dynamic_slice_in_dim(source, first_of((z + s) % groups), block, 0)
            came[s] = lax.ppermute(cut, "grp", [(i, (i + s) % groups) for i in range(groups)])

    head_moves(turned, early_shifts)
    later, share = lax.optimization_barrier((turned, share))
    head_moves(later, late_shifts)
    came[0] = lax.dynamic_slice_in_dim(later, start, block, 0)
    shares = traded(jnp.broadcast_to(share, (groups, *share.shape)), "grp")
    column, ints = shares[:, :here], shares[:, here : here + 2]
    column = column.reshape(tokens, part)
    y_at, x_at, core_at = j // 8, (j // 2) % 4, j % 2

    def moved(value, move):
        return lax.ppermute(value, "tp", [(i, move(i)) for i in range(lanes)])

    row = jnp.zeros((4, tokens, part), bf16)
    for s in range(4):
        came_x = moved(column, lambda i: i // 8 * 8 + (i % 8 + 2 * s) % 8) if s else column
        row = lax.dynamic_update_index_in_dim(row, came_x, (x_at - s) % 4, 0)
    pieces = [moved(row, lambda i: (i + 8 * s) % 32) if s else row for s in range(4)]
    pieces += [moved(piece, lambda i: i ^ 1) for piece in pieces]

    mine = tokens // lanes
    of_one_core = [[2 * i + core for i in range(lanes // 2)] for core in range(2)]
    in_smem = pl.BlockSpec(memory_space=pltpu.SMEM)
    in_vmem = pl.BlockSpec(memory_space=pltpu.VMEM)
    lhs, side = pl.pallas_call(
        lambda *refs: norm_kernel(*refs, width=width),
        out_shape=(
            jax.ShapeDtypeStruct((tokens + 2 * rank, width), bf16),
            jax.ShapeDtypeStruct((mine, 4 * rank), f32),
        ),
        in_specs=[in_smem, *vmem(3 + len(pieces))],
        out_specs=(in_vmem, in_vmem),
        scratch_shapes=[pltpu.VMEM((mine, width), bf16)],
        compiler_params=small,
    )(
        jnp.stack([y_at, core_at, j * mine]).astype(jnp.int32),
        norm_gain[None, :],
        proj_down.T,
        proj_hidden.T,
        *pieces,
    )

    ints = ints.astype(jnp.int32).reshape(groups, 2 * part)
    all_labels = ints[:, :here] + 128 * ints[:, here : 2 * here] + 16384 * ints[:, 2 * here : 3 * here]
    all_labels = all_labels.reshape(tokens, 1)
    all_lengths = ints[:, 3 * here : 3 * here + lengths.shape[0]].reshape(-1)
    spot = j * mine + lax.broadcasted_iota(jnp.int32, (mine, 1), 0)
    own_length = lax.dynamic_slice_in_dim(all_lengths, j * (mine // seq_span), mine // seq_span, 0)
    valid = (spot % seq_span < jnp.repeat(own_length, seq_span)[:, None]).astype(jnp.int32)
    ffn = jnp.dot(ffn_act, proj_ffn, preferred_element_type=f32)
    ffn = jnp.concatenate([jnp.zeros_like(ffn), ffn], axis=1)
    vocab_turned = lax.dynamic_slice_in_dim(proj_vocab, start, block, 0).T

    sums = None
    shifts = (0, *early_shifts, *late_shifts)
    for s in shifts[:-2]:
        depth = lax.dynamic_slice_in_dim(lhs, ((z - s) % groups) * rows_owned, rows_owned, 1)
        term = lax.dot_general(depth, came[s], by_last, preferred_element_type=f32)
        sums = term if sums is None else sums + term
    last = shifts[-2:]
    info = [j * vocab_owned + start, skipped, z * here, core_at]
    info = jnp.stack([*info, *(((z - s) % groups) * rows_owned for s in last)]).astype(jnp.int32)
    by_core = (lanes // 2, mine, 6 * rank)
    keep, send = pl.pallas_call(
        soft_kernel,
        out_shape=(jax.ShapeDtypeStruct(by_core, f32), jax.ShapeDtypeStruct(by_core, f32)),
        in_specs=[in_smem, *vmem(7)],
        out_specs=(in_vmem, in_vmem),
        scratch_shapes=[pltpu.VMEM((tokens, 6 * rank), f32)],
        compiler_params=small,
    )(info, sums, lhs, came[last[0]], came[last[1]], vocab_turned, all_labels, ffn)
    packed = pl.pallas_call(
        pair_merge_kernel,
        out_shape=jax.ShapeDtypeStruct(by_core, f32),
        in_specs=vmem(2),
        out_specs=in_vmem,
        compiler_params=small,
    )(keep, moved(send, lambda i: i ^ 1))
    packed = traded(packed, "tp", of_one_core)
    packed = pl.pallas_call(
        first_merge_kernel,
        out_shape=jax.ShapeDtypeStruct((groups, mine, 6 * rank), f32),
        in_specs=vmem(1),
        out_specs=in_vmem,
        compiler_params=small,
    )(packed)
    packed = traded(packed, "grp")
    sides = pl.pallas_call(
        lambda *refs: last_merge_kernel(*refs, width=width),
        out_shape=jax.ShapeDtypeStruct((lanes, mine, 2 * rank), bf16),
        in_specs=vmem(3),
        out_specs=in_vmem,
        compiler_params=small,
    )(packed, side, valid)
    sides = traded(sides, "tp").reshape(tokens, 2 * rank)

    stored, features = store.shape
    queries = tokens // seq_span
    per = features // rank
    query = pl.pallas_call(
        lambda *refs: query_kernel(*refs, span=seq_span),
        out_shape=jax.ShapeDtypeStruct((queries, features), bf16),
        in_specs=[in_smem, *vmem(1)],
        out_specs=in_vmem,
        compiler_params=small,
    )(jnp.stack([j % (lanes // 2) * per, queries // lanes, core_at]).astype(jnp.int32), sides)
    partial = lax.dot_general(query, store, by_last, preferred_element_type=f32)
    half = queries // 2
    other = moved(partial[half:].astype(bf16), lambda i: i ^ 1)
    partial = (partial[:half] + other.astype(f32)).astype(bf16)
    partial = traded(partial.reshape(lanes // 2, queries // lanes, stored), "tp", of_one_core)
    return jnp.sum(partial.astype(f32), axis=0)


def solution(mesh):
    return jax.shard_map(
        per_device,
        mesh=mesh,
        in_specs=(
            P("grp", None),
            P(),
            P("grp", "tp"),
            P("grp", "tp"),
            P("grp"),
            P("grp"),
            P(),
            P("tp", None),
            P("tp", None),
            P(),
            P("grp", "tp"),
        ),
        out_specs=P("tp", "grp"),
        check_vma=False,
    )
```

```python
import jax
import jax.numpy as jnp
from jax import lax
from jax.experimental import pallas as pl
from jax.experimental.pallas import tpu as pltpu
from jax.sharding import PartitionSpec as P


epsilon = 1e-05
f32 = jnp.float32
bf16 = jnp.bfloat16
by_last = (((1,), (1,)), ((), ()))

early_shifts = (1, 7)
late_shifts = (4, 3, 5, 2, 6)


small = pltpu.CompilerParams(vmem_limit_bytes=16 * 1024 * 1024)


def vmem(count):
    return [pl.BlockSpec(memory_space=pltpu.VMEM)] * count


def traded(value, axis, groups=None):
    return lax.all_to_all(
        value, axis, split_axis=0, concat_axis=0, tiled=True, axis_index_groups=groups
    )


def norm_kernel(info, gain_ref, down_ref, hidden_proj_ref, *refs, width):
    pieces, (lhs_ref, side_ref, own_ref) = refs[:-3], refs[-3:]
    xs, tokens, lane = pieces[0].shape
    rank = down_ref.shape[0]
    mine = side_ref.shape[0]
    rows = 64
    half = len(pieces) // 2
    places = []
    for n in range(len(pieces)):
        y = lax.rem(info[0] + half - n % half, half)
        core = info[1] if n < half else 1 - info[1]
        for x in range(xs):
            places.append((n, x, pl.multiple_of(((y * xs + x) * 2 + core) * lane, lane)))

    @pl.loop(0, tokens // rows)
    def _(i):
        at = pl.ds(pl.multiple_of(i * rows, rows), rows)
        squares = jnp.zeros((rows, lane), f32)
        for n, x, _ in places:
            value = pieces[n][x, at, :].astype(f32)
            squares += value * value
        mean = jnp.sum(squares, axis=1, keepdims=True) / width
        inverse = jnp.broadcast_to(lax.rsqrt(mean + epsilon), (rows, lane))
        for n, x, place in places:
            value = pieces[n][x, at, :].astype(f32)
            lhs_ref[at, pl.ds(place, lane)] = (gain_ref[:, pl.ds(place, lane)] * (value * inverse)).astype(bf16)

    gained = gain_ref[...] * down_ref[...].astype(f32)
    high = gained.astype(bf16)
    lhs_ref[tokens : tokens + rank] = high
    lhs_ref[tokens + rank :] = (gained - high.astype(f32)).astype(bf16)
    own = pl.ds(pl.multiple_of(info[2], mine), mine)
    squares = jnp.zeros((mine, lane), f32)
    for n, x, place in places:
        value = pieces[n][x, own, :]
        own_ref[:, pl.ds(place, lane)] = value
        squares += value.astype(f32) * value.astype(f32)
    inverse = lax.rsqrt(jnp.sum(squares, axis=1, keepdims=True) / width + epsilon)
    unit_down = inverse * lax.dot_general(own_ref[...], down_ref[...], by_last, preferred_element_type=f32)
    hidden_side = lax.dot_general(
        lhs_ref[own, :], hidden_proj_ref[...], by_last, preferred_element_type=f32
    )
    side_ref[:, :rank] = unit_down
    side_ref[:, rank : 2 * rank] = hidden_side
    side_ref[:, 2 * rank :] = jnp.broadcast_to(inverse, (mine, side_ref.shape[1] - 2 * rank))


def soft_kernel(
    info, sums_ref, lhs_ref, first_ref, last_ref, vocab_ref, label_ref, ffn_ref, keep_ref, send_ref,
    logits_ref, rows_ref, stats_ref,
):
    tokens, rank = label_ref.shape[0], vocab_ref.shape[0]
    columns, depth = last_ref.shape
    total = sums_ref[...]
    for n, ref in enumerate((first_ref, last_ref)):
        at = pl.ds(pl.multiple_of(info[4 + n], depth), depth)
        total += lax.dot_general(lhs_ref[:, at], ref[...], by_last, preferred_element_type=f32)
    logits_ref[...] = total
    fold = logits_ref[tokens : tokens + rank] + logits_ref[tokens + rank :]
    fold_high = fold.astype(bf16)
    fold_low = (fold - fold_high.astype(f32)).astype(bf16)
    right = jnp.concatenate([vocab_ref[...], fold_high, fold_low, fold_low], axis=0)
    spot = lax.broadcasted_iota(jnp.int32, (1, columns), 1)
    counted = spot >= info[1]
    count = 64
    lane = lax.broadcasted_iota(jnp.int32, (count, 2 * rank), 1)
    for first in range(0, tokens, count):
        rows = slice(first, first + count)
        logits = logits_ref[rows]
        peak = jnp.max(jnp.where(counted, logits, -jnp.inf), axis=1, keepdims=True)
        grown = jnp.where(counted, jnp.exp(jnp.minimum(logits - peak, 0.0)), 0.0)
        total = jnp.sum(grown, axis=1, keepdims=True)
        rounded = grown.astype(bf16)
        hit = counted & (label_ref[rows] == spot + info[0])
        dot_all = jnp.sum(rounded.astype(f32) * logits, axis=1, keepdims=True)
        dot_hit = jnp.sum(jnp.where(hit, logits, 0.0), axis=1, keepdims=True)
        rows_ref[rows] = rounded
        rows_ref[tokens + first : tokens + first + count] = hit.astype(f32).astype(bf16)
        stats = jnp.where(lane == 0, peak, jnp.where(lane == 1, total, jnp.where(lane == 2, dot_all, dot_hit)))
        stats_ref[rows] = jnp.where(lane < 4, stats, 0.0)
    here = ffn_ref.shape[0]
    own = pl.ds(pl.multiple_of(info[2], here), here)
    lane = lax.broadcasted_iota(jnp.int32, (here, 2 * rank), 1)
    stats_ref[own] = jnp.where(lane < rank, stats_ref[own], ffn_ref[...])
    both = lax.dot_general(rows_ref[...], right, by_last, preferred_element_type=f32)
    lane = lax.broadcasted_iota(jnp.int32, (1, 2 * rank), 1)
    both = both[:, : 2 * rank] + jnp.where(lane >= rank, both[:, 2 * rank :], 0.0)
    soft, mark = both[:tokens], both[tokens:]
    mine = keep_ref.shape[1]
    for core in range(2):

        @pl.when(info[3] == core)
        def _():
            for pair in range(keep_ref.shape[0]):
                for ref, place in ((keep_ref, 2 * pair + core), (send_ref, 2 * pair + 1 - core)):
                    rows = slice(mine * place, mine * (place + 1))
                    ref[pair, :, : 2 * rank] = soft[rows]
                    ref[pair, :, 2 * rank : 4 * rank] = mark[rows]
                    ref[pair, :, 4 * rank :] = stats_ref[rows]


def merged(x):
    stats = x[:, :, 256:]
    peaks = stats[:, :, 0:1]
    peak = jnp.max(peaks, axis=0)
    weight = jnp.exp(peaks - peak)
    soft = jnp.sum(x[:, :, :128] * weight, axis=0)
    mark = jnp.sum(x[:, :, 128:256], axis=0)
    lane = lax.broadcasted_iota(jnp.int32, stats.shape[1:], 1)
    scaled = jnp.sum(stats * weight, axis=0)
    plain = jnp.sum(stats, axis=0)
    kept = jnp.where(lane == 0, peak, jnp.where(lane < 3, scaled, plain))
    return soft, mark, kept


def pair_merge_kernel(keep_ref, came_ref, out_ref):
    for n in range(out_ref.shape[0]):
        soft, mark, kept = merged(jnp.stack([keep_ref[n], came_ref[n]]))
        out_ref[n, :, :128] = soft
        out_ref[n, :, 128:256] = mark
        out_ref[n, :, 256:] = kept


def first_merge_kernel(x_ref, out_ref):
    soft, mark, kept = merged(x_ref[...])
    for copy in range(out_ref.shape[0]):
        out_ref[copy, :, :128] = soft
        out_ref[copy, :, 128:256] = mark
        out_ref[copy, :, 256:] = kept


def last_merge_kernel(x_ref, side_ref, valid_ref, out_ref, *, width):
    soft, mark, kept = merged(x_ref[...])
    total, dot_all, dot_hit = kept[:, 1:2], kept[:, 2:3], kept[:, 3:4]
    both = soft / total - mark
    label_dot = dot_all / total - dot_hit
    rank = both.shape[1] // 2
    inverse, valid = side_ref[:, 2 * rank : 2 * rank + 1], valid_ref[...] > 0
    down_side = inverse * (both[:, rank:] - (label_dot / width) * side_ref[:, :rank])
    head_side = jnp.where(valid, both[:, :rank], 0.0)
    down_side = jnp.where(valid, down_side, 0.0)
    first = jnp.concatenate([head_side, side_ref[:, rank : 2 * rank]], axis=1).astype(bf16)
    second = jnp.concatenate([down_side, kept[:, rank:]], axis=1).astype(bf16)
    half = out_ref.shape[0] // 2
    for copy in range(half):
        out_ref[copy] = first
        out_ref[half + copy] = second


def query_kernel(info, sides_ref, out_ref, *, span, each):
    rank = sides_ref.shape[1] // 2
    blocks = sides_ref.shape[0] // (each * span)
    sides = []
    for far in range(2):
        core = info[1] + far - 2 * info[1] * far
        for n in range(blocks // 2):
            start = pl.multiple_of((2 * n + core) * each * span, each * span)
            sides.append(sides_ref[pl.ds(start, each * span), :])
    sides = jnp.concatenate(sides, axis=0)
    features = out_ref.shape[1]
    column = lax.broadcasted_iota(jnp.int32, (2 * rank, features), 0)
    wanted = rank + info[0] + lax.broadcasted_iota(jnp.int32, (2 * rank, features), 1) // rank
    chosen = (column == wanted).astype(f32).astype(bf16)
    left = jnp.dot(sides, chosen, preferred_element_type=f32)
    right = sides[:, :rank].astype(f32)
    product = left * jnp.concatenate([right] * (features // rank), axis=1)
    out_ref[...] = jnp.sum(product.reshape(-1, span, features), axis=1).astype(bf16)


def per_device(
    hidden_in,
    norm_gain,
    head_weight,
    ffn_act,
    labels,
    lengths,
    proj_hidden,
    proj_vocab,
    proj_ffn,
    proj_down,
    store,
):
    here, width = hidden_in.shape
    rows_owned, vocab_owned = head_weight.shape
    rank = proj_hidden.shape[1]
    groups, lanes = lax.axis_size("grp"), lax.axis_size("tp")
    tokens = here * groups
    seq_span = here // lengths.shape[0]
    z, j = lax.axis_index("grp"), lax.axis_index("tp")

    block = -(-vocab_owned // (8 * groups)) * 8
    turned = head_weight.T

    def first_of(group):
        return jnp.minimum(block * group, vocab_owned - block)

    start = first_of(z)
    skipped = block * z - start

    part = width // lanes
    digits = [labels % 128, labels // 128 % 128, labels // 16384, lengths]
    digits = jnp.concatenate(digits).astype(bf16)
    digits = jnp.pad(digits, (0, 16 * part - digits.shape[0])).reshape(16, part)
    share = lax.dynamic_slice_in_dim(hidden_in, j * part, part, 1)
    share = jnp.concatenate([share, digits], axis=0)

    came = {}

    def head_moves(source, shifts):
        for s in shifts:
            cut = lax.dynamic_slice_in_dim(source, first_of((z + s) % groups), block, 0)
            came[s] = lax.ppermute(cut, "grp", [(i, (i + s) % groups) for i in range(groups)])

    head_moves(turned, early_shifts)
    later, share = lax.optimization_barrier((turned, share))
    head_moves(later, late_shifts)
    came[0] = lax.dynamic_slice_in_dim(later, start, block, 0)
    shares = traded(jnp.broadcast_to(share, (groups, *share.shape)), "grp")
    column, ints = shares[:, :here], shares[:, here : here + 2]
    column = column.reshape(tokens, part)
    y_at, x_at, core_at = j // 8, (j // 2) % 4, j % 2

    def moved(value, move):
        return lax.ppermute(value, "tp", [(i, move(i)) for i in range(lanes)])

    row = jnp.zeros((4, tokens, part), bf16)
    for s in range(4):
        came_x = moved(column, lambda i: i // 8 * 8 + (i % 8 + 2 * s) % 8) if s else column
        row = lax.dynamic_update_index_in_dim(row, came_x, (x_at - s) % 4, 0)
    pieces = [moved(row, lambda i: (i + 8 * s) % 32) if s else row for s in range(4)]
    pieces += [moved(piece, lambda i: i ^ 1) for piece in pieces]

    mine = tokens // lanes
    of_one_core = [[2 * i + core for i in range(lanes // 2)] for core in range(2)]
    in_smem = pl.BlockSpec(memory_space=pltpu.SMEM)
    in_vmem = pl.BlockSpec(memory_space=pltpu.VMEM)
    lhs, side = pl.pallas_call(
        lambda *refs: norm_kernel(*refs, width=width),
        out_shape=(
            jax.ShapeDtypeStruct((tokens + 2 * rank, width), bf16),
            jax.ShapeDtypeStruct((mine, 4 * rank), f32),
        ),
        in_specs=[in_smem, *vmem(3 + len(pieces))],
        out_specs=(in_vmem, in_vmem),
        scratch_shapes=[pltpu.VMEM((mine, width), bf16)],
        compiler_params=small,
    )(
        jnp.stack([y_at, core_at, j * mine]).astype(jnp.int32),
        norm_gain[None, :],
        proj_down.T,
        proj_hidden.T,
        *pieces,
    )

    ints = ints.astype(jnp.int32).reshape(groups, 2 * part)
    all_labels = ints[:, :here] + 128 * ints[:, here : 2 * here] + 16384 * ints[:, 2 * here : 3 * here]
    all_labels = all_labels.reshape(tokens, 1)
    all_lengths = ints[:, 3 * here : 3 * here + lengths.shape[0]].reshape(-1)
    spot = j * mine + lax.broadcasted_iota(jnp.int32, (mine, 1), 0)
    own_length = lax.dynamic_slice_in_dim(all_lengths, j * (mine // seq_span), mine // seq_span, 0)
    valid = (spot % seq_span < jnp.repeat(own_length, seq_span)[:, None]).astype(jnp.int32)
    ffn = jnp.dot(ffn_act, proj_ffn, preferred_element_type=f32)
    ffn = jnp.concatenate([jnp.zeros_like(ffn), ffn], axis=1)
    vocab_turned = lax.dynamic_slice_in_dim(proj_vocab, start, block, 0).T

    sums = None
    shifts = (0, *early_shifts, *late_shifts)
    for s in shifts[:-2]:
        depth = lax.dynamic_slice_in_dim(lhs, ((z - s) % groups) * rows_owned, rows_owned, 1)
        term = lax.dot_general(depth, came[s], by_last, preferred_element_type=f32)
        sums = term if sums is None else sums + term
    last = shifts[-2:]
    info = [j * vocab_owned + start, skipped, z * here, core_at]
    info = jnp.stack([*info, *(((z - s) % groups) * rows_owned for s in last)]).astype(jnp.int32)
    by_core = (lanes // 2, mine, 6 * rank)
    keep, send = pl.pallas_call(
        soft_kernel,
        out_shape=(jax.ShapeDtypeStruct(by_core, f32), jax.ShapeDtypeStruct(by_core, f32)),
        in_specs=[in_smem, *vmem(7)],
        out_specs=(in_vmem, in_vmem),
        scratch_shapes=[
            pltpu.VMEM((tokens + 2 * rank, block), f32),
            pltpu.VMEM((2 * tokens, block), bf16),
            pltpu.VMEM((tokens, 2 * rank), f32),
        ],
        compiler_params=small,
    )(info, sums, lhs, came[last[0]], came[last[1]], vocab_turned, all_labels, ffn)
    packed = pl.pallas_call(
        pair_merge_kernel,
        out_shape=jax.ShapeDtypeStruct(by_core, f32),
        in_specs=vmem(2),
        out_specs=in_vmem,
        compiler_params=small,
    )(keep, moved(send, lambda i: i ^ 1))
    packed = traded(packed, "tp", of_one_core)
    packed = pl.pallas_call(
        first_merge_kernel,
        out_shape=jax.ShapeDtypeStruct((groups, mine, 6 * rank), f32),
        in_specs=vmem(1),
        out_specs=in_vmem,
        compiler_params=small,
    )(packed)
    packed = traded(packed, "grp")
    sides = pl.pallas_call(
        lambda *refs: last_merge_kernel(*refs, width=width),
        out_shape=jax.ShapeDtypeStruct((lanes, mine, 2 * rank), bf16),
        in_specs=vmem(3),
        out_specs=in_vmem,
        compiler_params=small,
    )(packed, side, valid)
    sides = traded(sides, "tp").reshape(tokens, 2 * rank)

    stored, features = store.shape
    queries = tokens // seq_span
    per = features // rank
    query = pl.pallas_call(
        lambda *refs: query_kernel(*refs, span=seq_span, each=queries // lanes),
        out_shape=jax.ShapeDtypeStruct((queries, features), bf16),
        in_specs=[in_smem, *vmem(1)],
        out_specs=in_vmem,
        compiler_params=small,
    )(jnp.stack([j % (lanes // 2) * per, core_at]).astype(jnp.int32), sides)
    partial = lax.dot_general(query, store, by_last, preferred_element_type=f32)
    half = queries // 2
    other = moved(partial[half:].astype(bf16), lambda i: i ^ 1)
    partial = (partial[:half] + other.astype(f32)).astype(bf16)
    partial = traded(partial.reshape(lanes // 2, queries // lanes, stored), "tp", of_one_core)
    return jnp.sum(partial.astype(f32), axis=0)


def solution(mesh):
    return jax.shard_map(
        per_device,
        mesh=mesh,
        in_specs=(
            P("grp", None),
            P(),
            P("grp", "tp"),
            P("grp", "tp"),
            P("grp"),
            P("grp"),
            P(),
            P("tp", None),
            P("tp", None),
            P(),
            P("grp", "tp"),
        ),
        out_specs=P("tp", "grp"),
        check_vma=False,
    )
```

```python
import jax
import jax.numpy as jnp
from jax import lax
from jax.experimental import pallas as pl
from jax.experimental.pallas import tpu as pltpu
from jax.sharding import PartitionSpec as P


epsilon = 1e-05
f32 = jnp.float32
bf16 = jnp.bfloat16
by_last = (((1,), (1,)), ((), ()))

early_shifts = (1, 7)
late_shifts = (4, 3, 5, 2, 6)


small = pltpu.CompilerParams(vmem_limit_bytes=16 * 1024 * 1024)


def vmem(count):
    return [pl.BlockSpec(memory_space=pltpu.VMEM)] * count


def traded(value, axis, groups=None):
    return lax.all_to_all(
        value, axis, split_axis=0, concat_axis=0, tiled=True, axis_index_groups=groups
    )


def norm_kernel(info, valid_ref, gain_ref, down_ref, hidden_proj_ref, *refs, width):
    pieces, (lhs_ref, side_ref, own_ref) = refs[:-3], refs[-3:]
    xs, tokens, lane = pieces[0].shape
    rank = down_ref.shape[0]
    mine = side_ref.shape[0]
    rows = 64
    half = len(pieces) // 2
    places = []
    for n in range(len(pieces)):
        y = lax.rem(info[0] + half - n % half, half)
        core = info[1] if n < half else 1 - info[1]
        for x in range(xs):
            places.append((n, x, pl.multiple_of(((y * xs + x) * 2 + core) * lane, lane)))

    @pl.loop(0, tokens // rows)
    def _(i):
        at = pl.ds(pl.multiple_of(i * rows, rows), rows)
        squares = jnp.zeros((rows, lane), f32)
        for n, x, _ in places:
            value = pieces[n][x, at, :].astype(f32)
            squares += value * value
        mean = jnp.sum(squares, axis=1, keepdims=True) / width
        inverse = jnp.broadcast_to(lax.rsqrt(mean + epsilon), (rows, lane))
        for n, x, place in places:
            value = pieces[n][x, at, :].astype(f32)
            lhs_ref[at, pl.ds(place, lane)] = (gain_ref[:, pl.ds(place, lane)] * (value * inverse)).astype(bf16)

    gained = gain_ref[...] * down_ref[...].astype(f32)
    high = gained.astype(bf16)
    lhs_ref[tokens : tokens + rank] = high
    lhs_ref[tokens + rank :] = (gained - high.astype(f32)).astype(bf16)
    own = pl.ds(pl.multiple_of(info[2], mine), mine)
    squares = jnp.zeros((mine, lane), f32)
    for n, x, place in places:
        value = pieces[n][x, own, :]
        own_ref[:, pl.ds(place, lane)] = value
        squares += value.astype(f32) * value.astype(f32)
    inverse = lax.rsqrt(jnp.sum(squares, axis=1, keepdims=True) / width + epsilon)
    unit_down = inverse * lax.dot_general(own_ref[...], down_ref[...], by_last, preferred_element_type=f32)
    hidden_side = lax.dot_general(
        lhs_ref[own, :], hidden_proj_ref[...], by_last, preferred_element_type=f32
    )
    side_ref[:, :rank] = unit_down
    side_ref[:, rank : 2 * rank] = hidden_side
    side_ref[:, 2 * rank : 3 * rank] = jnp.broadcast_to(inverse, (mine, rank))
    side_ref[:, 3 * rank :] = jnp.broadcast_to(valid_ref[...], (mine, rank)).astype(f32)


def soft_kernel(
    info, sums_ref, lhs_ref, first_ref, last_ref, vocab_ref, label_ref, ffn_ref, keep_ref, send_ref,
    logits_ref, rows_ref, stats_ref,
):
    tokens, rank = label_ref.shape[0], vocab_ref.shape[0]
    columns, depth = last_ref.shape
    total = sums_ref[...]
    for n, ref in enumerate((first_ref, last_ref)):
        at = pl.ds(pl.multiple_of(info[6 + n], depth), depth)
        total += lax.dot_general(lhs_ref[:, at], ref[...], by_last, preferred_element_type=f32)
    logits_ref[...] = total
    fold = logits_ref[tokens : tokens + rank] + logits_ref[tokens + rank :]
    fold_high = fold.astype(bf16)
    fold_low = (fold - fold_high.astype(f32)).astype(bf16)
    right = jnp.concatenate([vocab_ref[...], fold_high, fold_low, fold_low], axis=0)
    spot = lax.broadcasted_iota(jnp.int32, (1, columns), 1)
    counted = spot >= info[4]
    count = 64
    lane = lax.broadcasted_iota(jnp.int32, (count, 2 * rank), 1)
    for first in range(0, tokens, count):
        rows = slice(first, first + count)
        logits = logits_ref[rows]
        peak = jnp.max(jnp.where(counted, logits, -jnp.inf), axis=1, keepdims=True)
        grown = jnp.where(counted, jnp.exp(jnp.minimum(logits - peak, 0.0)), 0.0)
        total = jnp.sum(grown, axis=1, keepdims=True)
        rounded = grown.astype(bf16)
        hit = counted & (label_ref[rows] == spot + info[3])
        dot_all = jnp.sum(rounded.astype(f32) * logits, axis=1, keepdims=True)
        dot_hit = jnp.sum(jnp.where(hit, logits, 0.0), axis=1, keepdims=True)
        rows_ref[rows] = rounded
        rows_ref[tokens + first : tokens + first + count] = hit.astype(f32).astype(bf16)
        stats = jnp.where(lane == 0, peak, jnp.where(lane == 1, total, jnp.where(lane == 2, dot_all, dot_hit)))
        stats_ref[rows] = jnp.where(lane < 4, stats, 0.0)
    here = ffn_ref.shape[0]
    own = pl.ds(pl.multiple_of(info[5], here), here)
    lane = lax.broadcasted_iota(jnp.int32, (here, 2 * rank), 1)
    stats_ref[own] = jnp.where(lane < rank, stats_ref[own], ffn_ref[...])
    both = lax.dot_general(rows_ref[...], right, by_last, preferred_element_type=f32)
    lane = lax.broadcasted_iota(jnp.int32, (1, 2 * rank), 1)
    both = both[:, : 2 * rank] + jnp.where(lane >= rank, both[:, 2 * rank :], 0.0)
    soft, mark = both[:tokens], both[tokens:]
    mine = keep_ref.shape[1]
    for core in range(2):

        @pl.when(info[1] == core)
        def _():
            for pair in range(keep_ref.shape[0]):
                for ref, place in ((keep_ref, 2 * pair + core), (send_ref, 2 * pair + 1 - core)):
                    rows = slice(mine * place, mine * (place + 1))
                    ref[pair, :, : 2 * rank] = soft[rows]
                    ref[pair, :, 2 * rank : 4 * rank] = mark[rows]
                    ref[pair, :, 4 * rank :] = stats_ref[rows]


def merged(x):
    stats = x[:, :, 256:]
    peaks = stats[:, :, 0:1]
    peak = jnp.max(peaks, axis=0)
    weight = jnp.exp(peaks - peak)
    soft = jnp.sum(x[:, :, :128] * weight, axis=0)
    mark = jnp.sum(x[:, :, 128:256], axis=0)
    lane = lax.broadcasted_iota(jnp.int32, stats.shape[1:], 1)
    scaled = jnp.sum(stats * weight, axis=0)
    plain = jnp.sum(stats, axis=0)
    kept = jnp.where(lane == 0, peak, jnp.where(lane < 3, scaled, plain))
    return soft, mark, kept


def pair_merge_kernel(keep_ref, came_ref, out_ref):
    for n in range(out_ref.shape[0]):
        soft, mark, kept = merged(jnp.stack([keep_ref[n], came_ref[n]]))
        out_ref[n, :, :128] = soft
        out_ref[n, :, 128:256] = mark
        out_ref[n, :, 256:] = kept


def first_merge_kernel(x_ref, out_ref):
    soft, mark, kept = merged(x_ref[...])
    for copy in range(out_ref.shape[0]):
        out_ref[copy, :, :128] = soft
        out_ref[copy, :, 128:256] = mark
        out_ref[copy, :, 256:] = kept


def last_merge_kernel(x_ref, side_ref, out_ref, *, width):
    soft, mark, kept = merged(x_ref[...])
    total, dot_all, dot_hit = kept[:, 1:2], kept[:, 2:3], kept[:, 3:4]
    both = soft / total - mark
    label_dot = dot_all / total - dot_hit
    rank = both.shape[1] // 2
    inverse, valid = side_ref[:, 2 * rank : 2 * rank + 1], side_ref[:, 3 * rank : 3 * rank + 1] > 0.0
    down_side = inverse * (both[:, rank:] - (label_dot / width) * side_ref[:, :rank])
    head_side = jnp.where(valid, both[:, :rank], 0.0)
    down_side = jnp.where(valid, down_side, 0.0)
    first = jnp.concatenate([head_side, side_ref[:, rank : 2 * rank]], axis=1).astype(bf16)
    second = jnp.concatenate([down_side, kept[:, rank:]], axis=1).astype(bf16)
    half = out_ref.shape[0] // 2
    for copy in range(half):
        out_ref[copy] = first
        out_ref[half + copy] = second


def query_kernel(info, sides_ref, out_ref, *, span, each):
    rank = sides_ref.shape[1] // 2
    blocks = sides_ref.shape[0] // (each * span)
    sides = []
    for far in range(2):
        core = info[1] + far - 2 * info[1] * far
        for n in range(blocks // 2):
            start = pl.multiple_of((2 * n + core) * each * span, each * span)
            sides.append(sides_ref[pl.ds(start, each * span), :])
    sides = jnp.concatenate(sides, axis=0)
    features = out_ref.shape[1]
    column = lax.broadcasted_iota(jnp.int32, (2 * rank, features), 0)
    wanted = rank + info[8] + lax.broadcasted_iota(jnp.int32, (2 * rank, features), 1) // rank
    chosen = (column == wanted).astype(f32).astype(bf16)
    left = jnp.dot(sides, chosen, preferred_element_type=f32)
    right = sides[:, :rank].astype(f32)
    product = left * jnp.concatenate([right] * (features // rank), axis=1)
    out_ref[...] = jnp.sum(product.reshape(-1, span, features), axis=1).astype(bf16)


def per_device(
    hidden_in,
    norm_gain,
    head_weight,
    ffn_act,
    labels,
    lengths,
    proj_hidden,
    proj_vocab,
    proj_ffn,
    proj_down,
    store,
):
    here, width = hidden_in.shape
    rows_owned, vocab_owned = head_weight.shape
    rank = proj_hidden.shape[1]
    groups, lanes = lax.axis_size("grp"), lax.axis_size("tp")
    tokens = here * groups
    seq_span = here // lengths.shape[0]
    z, j = lax.axis_index("grp"), lax.axis_index("tp")

    block = -(-vocab_owned // (8 * groups)) * 8
    turned = head_weight.T

    def first_of(group):
        return jnp.minimum(block * group, vocab_owned - block)

    start = first_of(z)
    skipped = block * z - start

    part = width // lanes
    digits = [labels % 128, labels // 128 % 128, labels // 16384, lengths]
    digits = jnp.concatenate(digits).astype(bf16)
    digits = jnp.pad(digits, (0, 16 * part - digits.shape[0])).reshape(16, part)
    share = lax.dynamic_slice_in_dim(hidden_in, j * part, part, 1)
    share = jnp.concatenate([share, digits], axis=0)

    came = {}

    def head_moves(source, shifts):
        for s in shifts:
            cut = lax.dynamic_slice_in_dim(source, first_of((z + s) % groups), block, 0)
            came[s] = lax.ppermute(cut, "grp", [(i, (i + s) % groups) for i in range(groups)])

    head_moves(turned, early_shifts)
    later, share = lax.optimization_barrier((turned, share))
    head_moves(later, late_shifts)
    came[0] = lax.dynamic_slice_in_dim(later, start, block, 0)
    shares = traded(jnp.broadcast_to(share, (groups, *share.shape)), "grp")
    column, ints = shares[:, :here], shares[:, here : here + 2]
    column = column.reshape(tokens, part)
    y_at, x_at, core_at = j // 8, (j // 2) % 4, j % 2

    def moved(value, move):
        return lax.ppermute(value, "tp", [(i, move(i)) for i in range(lanes)])

    row = jnp.zeros((4, tokens, part), bf16)
    for s in range(4):
        came_x = moved(column, lambda i: i // 8 * 8 + (i % 8 + 2 * s) % 8) if s else column
        row = lax.dynamic_update_index_in_dim(row, came_x, (x_at - s) % 4, 0)
    pieces = [moved(row, lambda i: (i + 8 * s) % 32) if s else row for s in range(4)]
    pieces += [moved(piece, lambda i: i ^ 1) for piece in pieces]

    mine = tokens // lanes
    of_one_core = [[2 * i + core for i in range(lanes // 2)] for core in range(2)]
    ints = ints.astype(jnp.int32).reshape(groups, 2 * part)
    all_labels = ints[:, :here] + 128 * ints[:, here : 2 * here] + 16384 * ints[:, 2 * here : 3 * here]
    all_labels = all_labels.reshape(tokens, 1)
    all_lengths = ints[:, 3 * here : 3 * here + lengths.shape[0]].reshape(-1)
    spot = j * mine + lax.broadcasted_iota(jnp.int32, (mine, 1), 0)
    own_length = lax.dynamic_slice_in_dim(all_lengths, j * (mine // seq_span), mine // seq_span, 0)
    valid = (spot % seq_span < jnp.repeat(own_length, seq_span)[:, None]).astype(jnp.int32)
    shifts = (0, *early_shifts, *late_shifts)
    per = store.shape[1] // rank
    info = [y_at, core_at, j * mine, j * vocab_owned + start, skipped, z * here]
    info += [((z - s) % groups) * rows_owned for s in shifts[-2:]]
    info = jnp.stack([*info, j % (lanes // 2) * per]).astype(jnp.int32)
    in_smem = pl.BlockSpec(memory_space=pltpu.SMEM)
    in_vmem = pl.BlockSpec(memory_space=pltpu.VMEM)
    lhs, side = pl.pallas_call(
        lambda *refs: norm_kernel(*refs, width=width),
        out_shape=(
            jax.ShapeDtypeStruct((tokens + 2 * rank, width), bf16),
            jax.ShapeDtypeStruct((mine, 4 * rank), f32),
        ),
        in_specs=[in_smem, *vmem(4 + len(pieces))],
        out_specs=(in_vmem, in_vmem),
        scratch_shapes=[pltpu.VMEM((mine, width), bf16)],
        compiler_params=small,
    )(
        info,
        valid,
        norm_gain[None, :],
        proj_down.T,
        proj_hidden.T,
        *pieces,
    )

    ffn = jnp.dot(ffn_act, proj_ffn, preferred_element_type=f32)
    ffn = jnp.concatenate([jnp.zeros_like(ffn), ffn], axis=1)
    vocab_turned = lax.dynamic_slice_in_dim(proj_vocab, start, block, 0).T

    sums = None
    for s in shifts[:-2]:
        depth = lax.dynamic_slice_in_dim(lhs, ((z - s) % groups) * rows_owned, rows_owned, 1)
        term = lax.dot_general(depth, came[s], by_last, preferred_element_type=f32)
        sums = term if sums is None else sums + term
    by_core = (lanes // 2, mine, 6 * rank)
    keep, send = pl.pallas_call(
        soft_kernel,
        out_shape=(jax.ShapeDtypeStruct(by_core, f32), jax.ShapeDtypeStruct(by_core, f32)),
        in_specs=[in_smem, *vmem(7)],
        out_specs=(in_vmem, in_vmem),
        scratch_shapes=[
            pltpu.VMEM((tokens + 2 * rank, block), f32),
            pltpu.VMEM((2 * tokens, block), bf16),
            pltpu.VMEM((tokens, 2 * rank), f32),
        ],
        compiler_params=small,
    )(info, sums, lhs, came[shifts[-2]], came[shifts[-1]], vocab_turned, all_labels, ffn)
    packed = pl.pallas_call(
        pair_merge_kernel,
        out_shape=jax.ShapeDtypeStruct(by_core, f32),
        in_specs=vmem(2),
        out_specs=in_vmem,
        compiler_params=small,
    )(keep, moved(send, lambda i: i ^ 1))
    packed = traded(packed, "tp", of_one_core)
    packed = pl.pallas_call(
        first_merge_kernel,
        out_shape=jax.ShapeDtypeStruct((groups, mine, 6 * rank), f32),
        in_specs=vmem(1),
        out_specs=in_vmem,
        compiler_params=small,
    )(packed)
    packed = traded(packed, "grp")
    sides = pl.pallas_call(
        lambda *refs: last_merge_kernel(*refs, width=width),
        out_shape=jax.ShapeDtypeStruct((lanes, mine, 2 * rank), bf16),
        in_specs=vmem(2),
        out_specs=in_vmem,
        compiler_params=small,
    )(packed, side)
    sides = traded(sides, "tp").reshape(tokens, 2 * rank)

    stored, features = store.shape
    queries = tokens // seq_span
    query = pl.pallas_call(
        lambda *refs: query_kernel(*refs, span=seq_span, each=queries // lanes),
        out_shape=jax.ShapeDtypeStruct((queries, features), bf16),
        in_specs=[in_smem, *vmem(1)],
        out_specs=in_vmem,
        compiler_params=small,
    )(info, sides)
    partial = lax.dot_general(query, store, by_last, preferred_element_type=f32)
    half = queries // 2
    other = moved(partial[half:].astype(bf16), lambda i: i ^ 1)
    partial = (partial[:half] + other.astype(f32)).astype(bf16)
    partial = traded(partial.reshape(lanes // 2, queries // lanes, stored), "tp", of_one_core)
    return jnp.sum(partial.astype(f32), axis=0)


def solution(mesh):
    return jax.shard_map(
        per_device,
        mesh=mesh,
        in_specs=(
            P("grp", None),
            P(),
            P("grp", "tp"),
            P("grp", "tp"),
            P("grp"),
            P("grp"),
            P(),
            P("tp", None),
            P("tp", None),
            P(),
            P("grp", "tp"),
        ),
        out_specs=P("tp", "grp"),
        check_vma=False,
    )
```

```python
import jax
import jax.numpy as jnp
from jax import lax
from jax.experimental import pallas as pl
from jax.experimental.pallas import tpu as pltpu
from jax.sharding import PartitionSpec as P


epsilon = 1e-05
f32 = jnp.float32
bf16 = jnp.bfloat16
by_last = (((1,), (1,)), ((), ()))

early_shifts = (1, 7)
late_shifts = (4, 3, 5, 2, 6)


small = pltpu.CompilerParams(vmem_limit_bytes=16 * 1024 * 1024)


def vmem(count):
    return [pl.BlockSpec(memory_space=pltpu.VMEM)] * count


def traded(value, axis, groups=None):
    return lax.all_to_all(
        value, axis, split_axis=0, concat_axis=0, tiled=True, axis_index_groups=groups
    )


def norm_kernel(info, valid_ref, gain_ref, down_ref, hidden_proj_ref, *refs, width):
    pieces, (lhs_ref, side_ref, own_ref) = refs[:-3], refs[-3:]
    xs, tokens, lane = pieces[0].shape
    rank = down_ref.shape[0]
    mine = side_ref.shape[0]
    rows = 64
    half = len(pieces) // 2
    places = []
    for n in range(len(pieces)):
        y = lax.rem(info[0] + half - n % half, half)
        core = info[1] if n < half else 1 - info[1]
        for x in range(xs):
            places.append((n, x, pl.multiple_of(((y * xs + x) * 2 + core) * lane, lane)))

    @pl.loop(0, tokens // rows)
    def _(i):
        at = pl.ds(pl.multiple_of(i * rows, rows), rows)
        squares = jnp.zeros((rows, lane), f32)
        for n, x, _ in places:
            value = pieces[n][x, at, :].astype(f32)
            squares += value * value
        mean = jnp.sum(squares, axis=1, keepdims=True) / width
        inverse = jnp.broadcast_to(lax.rsqrt(mean + epsilon), (rows, lane))
        for n, x, place in places:
            value = pieces[n][x, at, :].astype(f32)
            lhs_ref[at, pl.ds(place, lane)] = (gain_ref[:, pl.ds(place, lane)] * (value * inverse)).astype(bf16)

    gained = gain_ref[...] * down_ref[...].astype(f32)
    high = gained.astype(bf16)
    lhs_ref[tokens : tokens + rank] = high
    lhs_ref[tokens + rank :] = (gained - high.astype(f32)).astype(bf16)
    own = pl.ds(pl.multiple_of(info[2], mine), mine)
    squares = jnp.zeros((mine, lane), f32)
    for n, x, place in places:
        value = pieces[n][x, own, :]
        own_ref[:, pl.ds(place, lane)] = value
        squares += value.astype(f32) * value.astype(f32)
    inverse = lax.rsqrt(jnp.sum(squares, axis=1, keepdims=True) / width + epsilon)
    unit_down = inverse * lax.dot_general(own_ref[...], down_ref[...], by_last, preferred_element_type=f32)
    hidden_side = lax.dot_general(
        lhs_ref[own, :], hidden_proj_ref[...], by_last, preferred_element_type=f32
    )
    side_ref[:, :rank] = unit_down
    side_ref[:, rank : 2 * rank] = hidden_side
    side_ref[:, 2 * rank : 3 * rank] = jnp.broadcast_to(inverse, (mine, rank))
    side_ref[:, 3 * rank :] = jnp.broadcast_to(valid_ref[...], (mine, rank)).astype(f32)


def soft_kernel(
    info, sums_ref, lhs_ref, first_ref, last_ref, vocab_ref, label_ref, ffn_ref, keep_ref, send_ref,
    logits_ref, rows_ref, stats_ref,
):
    tokens, rank = label_ref.shape[0], vocab_ref.shape[0]
    columns, depth = last_ref.shape
    total = sums_ref[...]
    for n, ref in enumerate((first_ref, last_ref)):
        at = pl.ds(pl.multiple_of(info[6 + n], depth), depth)
        total += lax.dot_general(lhs_ref[:, at], ref[...], by_last, preferred_element_type=f32)
    logits_ref[...] = total
    fold = logits_ref[tokens : tokens + rank] + logits_ref[tokens + rank :]
    fold_high = fold.astype(bf16)
    fold_low = (fold - fold_high.astype(f32)).astype(bf16)
    right = jnp.concatenate([vocab_ref[...], fold_high, fold_low, fold_low], axis=0)
    spot = lax.broadcasted_iota(jnp.int32, (1, columns), 1)
    counted = spot >= info[4]
    count = 64
    lane = lax.broadcasted_iota(jnp.int32, (count, 2 * rank), 1)
    for first in range(0, tokens, count):
        rows = slice(first, first + count)
        logits = logits_ref[rows]
        peak = jnp.max(jnp.where(counted, logits, -jnp.inf), axis=1, keepdims=True)
        grown = jnp.where(counted, jnp.exp(jnp.minimum(logits - peak, 0.0)), 0.0)
        total = jnp.sum(grown, axis=1, keepdims=True)
        rounded = grown.astype(bf16)
        hit = counted & (label_ref[rows] == spot + info[3])
        dot_all = jnp.sum(rounded.astype(f32) * logits, axis=1, keepdims=True)
        dot_hit = jnp.sum(jnp.where(hit, logits, 0.0), axis=1, keepdims=True)
        rows_ref[rows] = rounded
        rows_ref[tokens + first : tokens + first + count] = hit.astype(f32).astype(bf16)
        stats = jnp.where(lane == 0, peak, jnp.where(lane == 1, total, jnp.where(lane == 2, dot_all, dot_hit)))
        stats_ref[rows] = jnp.where(lane < 4, stats, 0.0)
    here = ffn_ref.shape[0]
    own = pl.ds(pl.multiple_of(info[5], here), here)
    lane = lax.broadcasted_iota(jnp.int32, (here, 2 * rank), 1)
    stats_ref[own] = jnp.where(lane < rank, stats_ref[own], ffn_ref[...])
    both = lax.dot_general(rows_ref[...], right, by_last, preferred_element_type=f32)
    lane = lax.broadcasted_iota(jnp.int32, (1, 2 * rank), 1)
    both = both[:, : 2 * rank] + jnp.where(lane >= rank, both[:, 2 * rank :], 0.0)
    soft, mark = both[:tokens], both[tokens:]
    mine = keep_ref.shape[1]
    for core in range(2):

        @pl.when(info[1] == core)
        def _():
            for pair in range(keep_ref.shape[0]):
                for ref, place in ((keep_ref, 2 * pair + core), (send_ref, 2 * pair + 1 - core)):
                    rows = slice(mine * place, mine * (place + 1))
                    ref[pair, :, : 2 * rank] = soft[rows]
                    ref[pair, :, 2 * rank : 4 * rank] = mark[rows]
                    ref[pair, :, 4 * rank :] = stats_ref[rows]


def merged(x):
    stats = x[:, :, 256:]
    peaks = stats[:, :, 0:1]
    peak = jnp.max(peaks, axis=0)
    weight = jnp.exp(peaks - peak)
    soft = jnp.sum(x[:, :, :128] * weight, axis=0)
    mark = jnp.sum(x[:, :, 128:256], axis=0)
    lane = lax.broadcasted_iota(jnp.int32, stats.shape[1:], 1)
    scaled = jnp.sum(stats * weight, axis=0)
    plain = jnp.sum(stats, axis=0)
    kept = jnp.where(lane == 0, peak, jnp.where(lane < 3, scaled, plain))
    return soft, mark, kept


def pair_merge_kernel(keep_ref, came_ref, out_ref):
    for n in range(out_ref.shape[0]):
        soft, mark, kept = merged(jnp.stack([keep_ref[n], came_ref[n]]))
        out_ref[n, :, :128] = soft
        out_ref[n, :, 128:256] = mark
        out_ref[n, :, 256:] = kept


def first_merge_kernel(x_ref, out_ref):
    soft, mark, kept = merged(x_ref[...])
    for copy in range(out_ref.shape[0]):
        out_ref[copy, :, :128] = soft
        out_ref[copy, :, 128:256] = mark
        out_ref[copy, :, 256:] = kept


def last_merge_kernel(x_ref, side_ref, out_ref, *, width):
    soft, mark, kept = merged(x_ref[...])
    total, dot_all, dot_hit = kept[:, 1:2], kept[:, 2:3], kept[:, 3:4]
    both = soft / total - mark
    label_dot = dot_all / total - dot_hit
    rank = both.shape[1] // 2
    inverse, valid = side_ref[:, 2 * rank : 2 * rank + 1], side_ref[:, 3 * rank : 3 * rank + 1] > 0.0
    down_side = inverse * (both[:, rank:] - (label_dot / width) * side_ref[:, :rank])
    head_side = jnp.where(valid, both[:, :rank], 0.0)
    down_side = jnp.where(valid, down_side, 0.0)
    first = jnp.concatenate([head_side, side_ref[:, rank : 2 * rank]], axis=1).astype(bf16)
    second = jnp.concatenate([down_side, kept[:, rank:]], axis=1).astype(bf16)
    half = out_ref.shape[0] // 2
    for copy in range(half):
        out_ref[copy] = first
        out_ref[half + copy] = second


def query_kernel(info, sides_ref, out_ref, *, span, each):
    rank = sides_ref.shape[1] // 2
    blocks = sides_ref.shape[0] // (each * span)
    sides = []
    for far in range(2):
        core = info[1] + far - 2 * info[1] * far
        for n in range(blocks // 2):
            start = pl.multiple_of((2 * n + core) * each * span, each * span)
            sides.append(sides_ref[pl.ds(start, each * span), :])
    sides = jnp.concatenate(sides, axis=0)
    features = out_ref.shape[1]
    column = lax.broadcasted_iota(jnp.int32, (2 * rank, features), 0)
    spot = lax.broadcasted_iota(jnp.int32, (2 * rank, features), 1)
    chosen = (column == rank + info[8] + spot // rank).astype(f32).astype(bf16)
    spread = (column == lax.rem(spot, rank)).astype(f32).astype(bf16)
    left = jnp.dot(sides, chosen, preferred_element_type=f32)
    right = jnp.dot(sides, spread, preferred_element_type=f32)
    product = left * right
    out_ref[...] = jnp.sum(product.reshape(-1, span, features), axis=1).astype(bf16)


def per_device(
    hidden_in,
    norm_gain,
    head_weight,
    ffn_act,
    labels,
    lengths,
    proj_hidden,
    proj_vocab,
    proj_ffn,
    proj_down,
    store,
):
    here, width = hidden_in.shape
    rows_owned, vocab_owned = head_weight.shape
    rank = proj_hidden.shape[1]
    groups, lanes = lax.axis_size("grp"), lax.axis_size("tp")
    tokens = here * groups
    seq_span = here // lengths.shape[0]
    z, j = lax.axis_index("grp"), lax.axis_index("tp")

    block = -(-vocab_owned // (8 * groups)) * 8
    turned = head_weight.T

    def first_of(group):
        return jnp.minimum(block * group, vocab_owned - block)

    start = first_of(z)
    skipped = block * z - start

    part = width // lanes
    digits = [labels % 128, labels // 128 % 128, labels // 16384, lengths]
    digits = jnp.concatenate(digits).astype(bf16)
    digits = jnp.pad(digits, (0, 16 * part - digits.shape[0])).reshape(16, part)
    share = lax.dynamic_slice_in_dim(hidden_in, j * part, part, 1)
    share = jnp.concatenate([share, digits], axis=0)

    came = {}

    def head_moves(source, shifts):
        for s in shifts:
            cut = lax.dynamic_slice_in_dim(source, first_of((z + s) % groups), block, 0)
            came[s] = lax.ppermute(cut, "grp", [(i, (i + s) % groups) for i in range(groups)])

    head_moves(turned, early_shifts)
    later, share = lax.optimization_barrier((turned, share))
    head_moves(later, late_shifts)
    came[0] = lax.dynamic_slice_in_dim(later, start, block, 0)
    shares = traded(jnp.broadcast_to(share, (groups, *share.shape)), "grp")
    column, ints = shares[:, :here], shares[:, here : here + 2]
    column = column.reshape(tokens, part)
    y_at, x_at, core_at = j // 8, (j // 2) % 4, j % 2

    def moved(value, move):
        return lax.ppermute(value, "tp", [(i, move(i)) for i in range(lanes)])

    row = jnp.zeros((4, tokens, part), bf16)
    for s in range(4):
        came_x = moved(column, lambda i: i // 8 * 8 + (i % 8 + 2 * s) % 8) if s else column
        row = lax.dynamic_update_index_in_dim(row, came_x, (x_at - s) % 4, 0)
    pieces = [moved(row, lambda i: (i + 8 * s) % 32) if s else row for s in range(4)]
    pieces += [moved(piece, lambda i: i ^ 1) for piece in pieces]

    mine = tokens // lanes
    of_one_core = [[2 * i + core for i in range(lanes // 2)] for core in range(2)]
    ints = ints.astype(jnp.int32).reshape(groups, 2 * part)
    all_labels = ints[:, :here] + 128 * ints[:, here : 2 * here] + 16384 * ints[:, 2 * here : 3 * here]
    all_labels = all_labels.reshape(tokens, 1)
    all_lengths = ints[:, 3 * here : 3 * here + lengths.shape[0]].reshape(-1)
    spot = j * mine + lax.broadcasted_iota(jnp.int32, (mine, 1), 0)
    own_length = lax.dynamic_slice_in_dim(all_lengths, j * (mine // seq_span), mine // seq_span, 0)
    valid = (spot % seq_span < jnp.repeat(own_length, seq_span)[:, None]).astype(jnp.int32)
    shifts = (0, *early_shifts, *late_shifts)
    per = store.shape[1] // rank
    info = [y_at, core_at, j * mine, j * vocab_owned + start, skipped, z * here]
    info += [((z - s) % groups) * rows_owned for s in shifts[-2:]]
    info = jnp.stack([*info, j % (lanes // 2) * per]).astype(jnp.int32)
    in_smem = pl.BlockSpec(memory_space=pltpu.SMEM)
    in_vmem = pl.BlockSpec(memory_space=pltpu.VMEM)
    lhs, side = pl.pallas_call(
        lambda *refs: norm_kernel(*refs, width=width),
        out_shape=(
            jax.ShapeDtypeStruct((tokens + 2 * rank, width), bf16),
            jax.ShapeDtypeStruct((mine, 4 * rank), f32),
        ),
        in_specs=[in_smem, *vmem(4 + len(pieces))],
        out_specs=(in_vmem, in_vmem),
        scratch_shapes=[pltpu.VMEM((mine, width), bf16)],
        compiler_params=small,
    )(
        info,
        valid,
        norm_gain[None, :],
        proj_down.T,
        proj_hidden.T,
        *pieces,
    )

    ffn = jnp.dot(ffn_act, proj_ffn, preferred_element_type=f32)
    ffn = jnp.concatenate([jnp.zeros_like(ffn), ffn], axis=1)
    vocab_turned = lax.dynamic_slice_in_dim(proj_vocab, start, block, 0).T

    sums = None
    for s in shifts[:-2]:
        depth = lax.dynamic_slice_in_dim(lhs, ((z - s) % groups) * rows_owned, rows_owned, 1)
        term = lax.dot_general(depth, came[s], by_last, preferred_element_type=f32)
        sums = term if sums is None else sums + term
    by_core = (lanes // 2, mine, 6 * rank)
    keep, send = pl.pallas_call(
        soft_kernel,
        out_shape=(jax.ShapeDtypeStruct(by_core, f32), jax.ShapeDtypeStruct(by_core, f32)),
        in_specs=[in_smem, *vmem(7)],
        out_specs=(in_vmem, in_vmem),
        scratch_shapes=[
            pltpu.VMEM((tokens + 2 * rank, block), f32),
            pltpu.VMEM((2 * tokens, block), bf16),
            pltpu.VMEM((tokens, 2 * rank), f32),
        ],
        compiler_params=small,
    )(info, sums, lhs, came[shifts[-2]], came[shifts[-1]], vocab_turned, all_labels, ffn)
    packed = pl.pallas_call(
        pair_merge_kernel,
        out_shape=jax.ShapeDtypeStruct(by_core, f32),
        in_specs=vmem(2),
        out_specs=in_vmem,
        compiler_params=small,
    )(keep, moved(send, lambda i: i ^ 1))
    packed = traded(packed, "tp", of_one_core)
    packed = pl.pallas_call(
        first_merge_kernel,
        out_shape=jax.ShapeDtypeStruct((groups, mine, 6 * rank), f32),
        in_specs=vmem(1),
        out_specs=in_vmem,
        compiler_params=small,
    )(packed)
    packed = traded(packed, "grp")
    sides = pl.pallas_call(
        lambda *refs: last_merge_kernel(*refs, width=width),
        out_shape=jax.ShapeDtypeStruct((lanes, mine, 2 * rank), bf16),
        in_specs=vmem(2),
        out_specs=in_vmem,
        compiler_params=small,
    )(packed, side)
    sides = traded(sides, "tp").reshape(tokens, 2 * rank)

    stored, features = store.shape
    queries = tokens // seq_span
    query = pl.pallas_call(
        lambda *refs: query_kernel(*refs, span=seq_span, each=queries // lanes),
        out_shape=jax.ShapeDtypeStruct((queries, features), bf16),
        in_specs=[in_smem, *vmem(1)],
        out_specs=in_vmem,
        compiler_params=small,
    )(info, sides)
    partial = lax.dot_general(query, store, by_last, preferred_element_type=f32)
    half = queries // 2
    other = moved(partial[half:].astype(bf16), lambda i: i ^ 1)
    partial = (partial[:half] + other.astype(f32)).astype(bf16)
    partial = traded(partial.reshape(lanes // 2, queries // lanes, stored), "tp", of_one_core)
    return jnp.sum(partial.astype(f32), axis=0)


def solution(mesh):
    return jax.shard_map(
        per_device,
        mesh=mesh,
        in_specs=(
            P("grp", None),
            P(),
            P("grp", "tp"),
            P("grp", "tp"),
            P("grp"),
            P("grp"),
            P(),
            P("tp", None),
            P("tp", None),
            P(),
            P("grp", "tp"),
        ),
        out_specs=P("tp", "grp"),
        check_vma=False,
    )
```
